32 devices in a mesh: tm: 16 (over z, y, x), tensor: 2 (over core).
Axes of the slice: x: 2, y: 2, z: 4, core: 2. Of those that a mesh axis runs over, the one named last changes fastest.
Arguments:
- noise_start: float32 [1, 16384], replicated, may hold values from -6 to 6
- timesteps: int32 [17], replicated, may hold values from 0 to 599, as said below
- class_labels: int32 [16, 1], P('tm'), may hold values from 0 to 999
- mixing: float32 [2, 16], P(None, 'tm'), may hold values from -0.5 to 0.5
- class_table: bfloat16 [1000, 768], replicated, may hold values from -3 to 3
- time_in: bfloat16 [256, 768], replicated, may hold values from -0.75 to 0.75
- time_out: bfloat16 [768, 768], replicated, may hold values from -0.21875 to 0.21875
- ada_weight: bfloat16 [768, 4608], replicated, may hold values from -0.21875 to 0.21875
- final_ada: bfloat16 [768, 1536], replicated, may hold values from -0.21875 to 0.21875
- patch_weight: bfloat16 [16, 768], replicated, may hold values from -1.5 to 1.5
- q_weight: bfloat16 [768, 768], replicated, may hold values from -1.5 to 1.5
- kv_weight: bfloat16 [768, 1536], replicated, may hold values from -1.5 to 1.5
- out_weight: bfloat16 [768, 768], replicated, may hold values from -0.4375 to 0.4375
- up_weight: bfloat16 [768, 3072], P(None, 'tensor'), may hold values from -0.21875 to 0.21875
- down_weight: bfloat16 [3072, 768], P('tensor'), may hold values from -0.21875 to 0.21875
- final_weight: bfloat16 [768, 16], replicated, may hold values from -0.21875 to 0.21875
Outputs:
- states: float32 [16, 1, 16384], P('tm')
- residuals: float32 [2, 16], P(None, 'tm')
The draws below stay inside these ranges and needn't reach their ends.
Inputs may be any that keep to these rules, and one draw needn't show every extreme that they name: `timesteps`: strictly decreasing; the first is 599, the last is 0, all others lie from 100 to 549.
All inputs are finite; a program needn't handle non-finite values.
Results may differ from the reference program's by a relative error of at most 0.008.
Values may be sent and summed in bfloat16 or wider, within the bound.
A program may use at most 128 MiB of HBM per device.

```python
import math
import jax
import jax.numpy as jnp
from jax import lax

D = 768
HEADS = 12
FF = 3072
SEQ = 1024
PATCH = 16
CLASSES = 1000
FREQ = 256
IMG = 1
ITERS = 2
WINDOW = 16
LAT = 16384
N_TENSOR = 2


def attention_pair(key):
    query_key = jax.random.fold_in(key, 101)
    other_key = jax.random.fold_in(key, 202)
    query_part = jax.random.normal(query_key, (D, D), jnp.float32) / jnp.sqrt(jnp.float32(D))
    key_part = jax.random.normal(other_key, (D, 2 * D), jnp.float32) / jnp.sqrt(jnp.float32(D))
    head_width = D // HEADS
    head_rank = jax.random.permutation(jax.random.fold_in(key, 303), HEADS)
    chosen = (head_rank < HEADS // 2).astype(jnp.float32)
    strength = 1.5
    column_head = jnp.arange(D, dtype=jnp.int32) // head_width
    column_match = (column_head[:, None] == jnp.arange(HEADS, dtype=jnp.int32)[None, :]).astype(jnp.float32)
    factor = strength * jnp.sum(column_match * chosen[None, :], axis=1)
    keys = key_part[:, :D] + factor[None, :] * query_part
    key_part = jnp.concatenate([keys, key_part[:, D:]], axis=1)
    return (jnp.clip(query_part, -1.5, 1.5), jnp.clip(key_part, -1.5, 1.5))


def draw_q_weight(key, part):
    return attention_pair(key)[0].astype(jnp.bfloat16)


def draw_kv_weight(key, part):
    return attention_pair(key)[1].astype(jnp.bfloat16)


def draw_timesteps(key, part):
    chosen = jax.random.permutation(key, 450)[:WINDOW - 1].astype(jnp.int32) + 100
    lower = -jnp.sort(-chosen)
    return jnp.concatenate([jnp.full((1,), 599, jnp.int32), lower, jnp.zeros((1,), jnp.int32)])


def plant(entries, key, low, high):
    place = [jax.random.randint(jax.random.fold_in(key, axis), (), 0, length) for axis, length in enumerate(entries.shape)]
    longest = entries.shape.index(max(entries.shape))
    beside = place[:longest] + [(place[longest] + 1) % entries.shape[longest]] + place[longest + 1:]
    return entries.at[tuple(place)].set(low).at[tuple(beside)].set(high)


def block_scale(rng, shape, shards, least, largest):
    gain = 1.0
    for axis_at, parts in shards:
        steps = jax.random.uniform(jax.random.fold_in(jax.random.fold_in(rng, 6), axis_at), (parts,), jnp.float32, least / len(shards), largest / len(shards))
        gain = gain * jnp.repeat(jnp.exp(steps), shape[axis_at] // parts).reshape((-1,) + (1,) * (len(shape) - 1 - axis_at))
    return gain


def gaussian(stream_key, extent, scale, reach, shards=(), kind=jnp.bfloat16):
    factor_of = block_scale(stream_key, extent, shards, -0.22, 0.18) if shards else 1.0
    result = jax.random.normal(stream_key, extent, jnp.float32) * scale * factor_of
    return jnp.minimum(jnp.maximum(result, -reach), reach).astype(kind)


def setup_inputs(seed: int = 0) -> dict:
    seeds = jax.random.split(jax.random.key(seed), 17)
    noise_start = gaussian(seeds[0], (IMG, LAT), 1.0, 6.0, (), jnp.float32)
    timesteps = draw_timesteps(jax.random.fold_in(seeds[16], 71), 0)
    class_labels = plant(jax.random.randint(seeds[2], (WINDOW, IMG), 0, CLASSES), jax.random.fold_in(seeds[2], 1), 0, CLASSES - 1).astype(jnp.int32)
    mixing = jnp.clip(jax.random.uniform(seeds[3], (ITERS, WINDOW), jnp.float32, -0.5, 0.5) * block_scale(seeds[3], (ITERS, WINDOW), ((1, 16),), -0.4, 0.0), -0.5, 0.5)
    class_table = gaussian(seeds[4], (CLASSES, D), 0.5, 3.0)
    time_in = gaussian(seeds[5], (FREQ, D), (FREQ // 4) ** -0.5, 0.75)
    time_out = gaussian(seeds[6], (D, D), D ** -0.5, 0.21875)
    ada_weight = gaussian(seeds[7], (D, 6 * D), D ** -0.5, 0.21875)
    final_ada = gaussian(seeds[8], (D, 2 * D), D ** -0.5, 0.21875)
    patch_weight = gaussian(seeds[9], (PATCH, D), PATCH ** -0.5, 1.5)
    q_weight = draw_q_weight(jax.random.fold_in(seeds[16], 71), 0)
    kv_weight = draw_kv_weight(jax.random.fold_in(seeds[16], 71), 0)
    out_weight = gaussian(seeds[12], (D, D), (D // 4) ** -0.5, 0.4375)
    up_weight = gaussian(seeds[13], (D, FF), D ** -0.5, 0.21875, ((1, 2),))
    down_weight = gaussian(seeds[14], (FF, D), (FF // 4) ** -0.5, 0.21875, ((0, 2),))
    final_weight = gaussian(seeds[15], (D, PATCH), D ** -0.5, 0.21875)
    return {"noise_start": noise_start, "timesteps": timesteps, "class_labels": class_labels, "mixing": mixing, "class_table": class_table, "time_in": time_in, "time_out": time_out, "ada_weight": ada_weight, "final_ada": final_ada, "patch_weight": patch_weight, "q_weight": q_weight, "kv_weight": kv_weight, "out_weight": out_weight, "up_weight": up_weight, "down_weight": down_weight, "final_weight": final_weight}


norm_eps = 1e-06
plan_steps = 1000

def log_table():
    levels = jnp.arange(plan_steps, dtype=jnp.float32)
    beta_values = 0.0001 + (0.02 - 0.0001) * levels / (plan_steps - 1)
    return jnp.cumsum(jnp.log(1.0 - beta_values))

def alpha_at(moments):
    matches = moments[:, None] == jnp.arange(plan_steps, dtype=jnp.int32)[None, :]
    return jnp.exp(lax.optimization_barrier(jnp.sum(jnp.where(matches, log_table()[None, :], 0.0), axis=1)))

def time_features(moment):
    half_count = FREQ // 2
    freq_rates = jnp.exp(-math.log(10000.0) * jnp.arange(half_count, dtype=jnp.float32) / half_count)
    angles = moment.astype(jnp.float32) * freq_rates
    return jnp.concatenate([jnp.cos(angles), jnp.sin(angles)])[None, :]

def positions():
    half_width = D // 2
    places = jnp.arange(SEQ, dtype=jnp.float32)[:, None]
    freq_rates = jnp.exp(-math.log(10000.0) * jnp.arange(half_width, dtype=jnp.float32) / half_width)
    angles = places * freq_rates[None, :]
    return jnp.concatenate([jnp.sin(angles), jnp.cos(angles)], axis=1)

def layer_norm(values):
    center = values - lax.optimization_barrier(jnp.mean(values, axis=-1, keepdims=True))
    spread = lax.optimization_barrier(jnp.mean(center * center, axis=-1, keepdims=True))
    return center * lax.rsqrt(spread + norm_eps)

def modulate(values, shift, scale):
    return layer_norm(values) * (1.0 + scale) + shift

def split_rows(matrix, count):
    return [matrix[:, None, column * D:(column + 1) * D] for column in range(count)]

def condition(moment, labels, class_table, time_in, time_out, ada_weight, final_ada):
    features = time_features(moment).astype(jnp.bfloat16)
    time_hidden = jax.nn.silu(jnp.dot(features, time_in, preferred_element_type=jnp.float32)).astype(jnp.bfloat16)
    time_embed = jnp.dot(time_hidden, time_out, preferred_element_type=jnp.float32)
    onehot = (labels[:, None] == jnp.arange(CLASSES, dtype=jnp.int32)[None, :]).astype(jnp.bfloat16)
    classes = jnp.dot(onehot, class_table, preferred_element_type=jnp.float32)
    summed = jax.nn.silu(time_embed + classes).astype(jnp.bfloat16)
    modul = jnp.dot(summed, ada_weight, preferred_element_type=jnp.float32)
    final_mod = jnp.dot(summed, final_ada, preferred_element_type=jnp.float32)
    return (modul, final_mod)

def denoise(state_in, moment, labels, params):
    class_table, time_in, time_out, ada_weight, final_ada, patch_weight, q_weight, kv_weight, out_weight, up_weight, down_weight, final_weight = params
    modul, final_mod = condition(moment, labels, class_table, time_in, time_out, ada_weight, final_ada)
    shift_attn, scale_attn, gate_attn, shift_mlp, scale_mlp, gate_mlp = split_rows(modul, 6)
    shift_out, scale_out = split_rows(final_mod, 2)
    head_dim = D // HEADS
    tokens = state_in.astype(jnp.bfloat16).reshape(IMG * SEQ, PATCH)
    hidden = jnp.dot(tokens, patch_weight, preferred_element_type=jnp.float32).reshape(IMG, SEQ, D) + positions()[None]
    attn_in = modulate(hidden, shift_attn, scale_attn).astype(jnp.bfloat16).reshape(IMG * SEQ, D)
    queries = jnp.dot(attn_in, q_weight, preferred_element_type=jnp.float32).astype(jnp.bfloat16)
    queries = queries.reshape(IMG, SEQ, HEADS, head_dim)
    key_value = jnp.dot(attn_in, kv_weight, preferred_element_type=jnp.float32).astype(jnp.bfloat16)
    key_value = key_value.reshape(IMG, SEQ, 2 * D)
    key_heads = key_value[:, :, :D].reshape(IMG, SEQ, HEADS, head_dim)
    value_heads = key_value[:, :, D:].reshape(IMG, SEQ, HEADS, head_dim)
    scores = jnp.einsum('bqhd,bkhd->bhqk', queries.astype(jnp.float32), key_heads.astype(jnp.float32))
    scores = scores * (1.0 / math.sqrt(head_dim))
    attention = jax.nn.softmax(scores, axis=-1).astype(jnp.bfloat16)
    attended = jnp.einsum('bhqk,bkhd->bqhd', attention.astype(jnp.float32), value_heads.astype(jnp.float32))
    attended = attended.astype(jnp.bfloat16).reshape(IMG * SEQ, D)
    hidden = hidden + gate_attn * jnp.dot(attended, out_weight, preferred_element_type=jnp.float32).reshape(IMG, SEQ, D)
    mlp_in = modulate(hidden, shift_mlp, scale_mlp).astype(jnp.bfloat16).reshape(IMG * SEQ, D)
    lifted = jax.nn.gelu(jnp.dot(mlp_in, up_weight, preferred_element_type=jnp.float32), approximate=True)
    lifted = lifted.astype(jnp.bfloat16)
    width_part = FF // N_TENSOR
    mlp_total = jnp.zeros((IMG * SEQ, D), jnp.float32)
    for block_index in range(N_TENSOR):
        low = block_index * width_part
        partial_value = jnp.dot(lifted[:, low:low + width_part], down_weight[low:low + width_part], preferred_element_type=jnp.float32)
        mlp_total = mlp_total + lax.optimization_barrier(partial_value.astype(jnp.bfloat16)).astype(jnp.float32)
    hidden = hidden + gate_mlp * mlp_total.reshape(IMG, SEQ, D)
    final_in = modulate(hidden, shift_out, scale_out).astype(jnp.bfloat16).reshape(IMG * SEQ, D)
    return jnp.dot(final_in, final_weight, preferred_element_type=jnp.float32).reshape(IMG, LAT)

def reference(noise_start, timesteps, class_labels, mixing, class_table, time_in, time_out, ada_weight, final_ada, patch_weight, q_weight, kv_weight, out_weight, up_weight, down_weight, final_weight):
    params = (class_table, time_in, time_out, ada_weight, final_ada, patch_weight, q_weight, kv_weight, out_weight, up_weight, down_weight, final_weight)
    alphas = alpha_at(timesteps)
    alpha_now = alphas[:WINDOW]
    alpha_next = alphas[1:]
    keep_coef = jnp.sqrt(alpha_next / alpha_now)
    noise_coef = jnp.sqrt(1.0 - alpha_next) - jnp.sqrt(alpha_next * (1.0 - alpha_now) / alpha_now)
    states = jnp.broadcast_to(noise_start[None], (WINDOW, IMG, LAT))
    previous = states
    residual_rows = []
    for iteration in range(ITERS):
        inputs = jnp.concatenate([noise_start[None], states[:WINDOW - 1]], axis=0)
        predicted = lax.map(lambda packed: denoise(packed[0], packed[1], packed[2], params), (inputs, timesteps[:WINDOW], class_labels))
        drifts = (keep_coef - 1.0)[:, None, None] * inputs + noise_coef[:, None, None] * predicted
        picard_map = noise_start[None] + jnp.cumsum(drifts, axis=0)
        residual_rows.append(lax.optimization_barrier(jnp.mean(jnp.square(picard_map - states), axis=(1, 2))))
        mixed_states = picard_map + mixing[iteration][:, None, None] * (picard_map - previous)
        previous = picard_map
        states = mixed_states
    return (states, jnp.stack(residual_rows))
```

```python
import functools
import math

import jax
import jax.numpy as jnp
from jax import lax
from jax.experimental import pallas as pl
from jax.experimental.pallas import tpu as pltpu
from jax.sharding import PartitionSpec as P

HEAD_DIM = 64
ITERS = 2
PERIOD = 32
norm_eps = 1e-06
plan_steps = 1000
MESH = pl.DeviceIdType.MESH
F32 = jnp.float32
BF16 = jnp.bfloat16
ANY = pl.BlockSpec(memory_space=pl.ANY)
VM = pl.BlockSpec(memory_space=pltpu.VMEM)
SM = pl.BlockSpec(memory_space=pltpu.SMEM)
LIMIT = 56 * 1024 * 1024


def log_table():
    levels = jnp.arange(plan_steps, dtype=jnp.float32)
    beta_values = 0.0001 + (0.02 - 0.0001) * levels / (plan_steps - 1)
    return jnp.log(1.0 - beta_values)


def alpha_at(moments):
    reached = jnp.arange(plan_steps, dtype=jnp.int32)[None, :] <= moments[:, None]
    return jnp.exp(jnp.sum(jnp.where(reached, log_table()[None, :], 0.0), axis=1))


def time_features(moment, half_count):
    freq_rates = jnp.exp(
        -math.log(10000.0) * jnp.arange(half_count, dtype=jnp.float32) / half_count
    )
    angles = moment.astype(jnp.float32) * freq_rates
    return jnp.concatenate([jnp.cos(angles), jnp.sin(angles)])[None, :]


def pick_entry(vector, wanted):
    matches = jnp.arange(vector.shape[0], dtype=jnp.int32) == wanted
    return jnp.sum(jnp.where(matches, vector, 0))


def normed(values):
    center = values - jnp.mean(values, axis=-1, keepdims=True)
    spread = jnp.mean(center * center, axis=-1, keepdims=True)
    return center * lax.rsqrt(spread + norm_eps)


def attention_kernel(
    tile,
    x_ref,
    patch_ref,
    far_sin,
    far_cos,
    near_sin,
    near_cos,
    mod_ref,
    q_hbm,
    kv_hbm,
    out_hbm,
    h_ref,
    kv_s,
    q_s,
    att_s,
    q_w,
    kv_w,
    out_w,
    sems,
):
    rows_own, width = h_ref.shape
    seq = x_ref.shape[1]
    copies = [
        pltpu.make_async_copy(src, dst, sems.at[i])
        for i, (src, dst) in enumerate(((kv_hbm, kv_w), (q_hbm, q_w), (out_hbm, out_w)))
    ]
    for copy in copies:
        copy.start()
    shift, scale, gate = mod_ref[0:1, :], 1.0 + mod_ref[1:2, :], mod_ref[2:3, :]
    groups = tile // PERIOD

    def embed(t):
        rows = pl.ds(pl.multiple_of(t * tile, tile), tile)
        tokens = x_ref[:, rows].astype(BF16)
        hidden = lax.dot_general(
            tokens, patch_ref[...], (((0,), (0,)), ((), ())), preferred_element_type=F32
        )
        far = pl.ds(pl.multiple_of(t * groups, groups), groups)
        fs, fc = far_sin[far, :][:, None, :], far_cos[far, :][:, None, :]
        ns, nc = near_sin[...][None], near_cos[...][None]
        sines = (fs * nc + fc * ns).reshape(tile, width // 2)
        cosines = (fc * nc - fs * ns).reshape(tile, width // 2)
        hidden = hidden + jnp.concatenate([sines, cosines], axis=1)
        return rows, hidden, (normed(hidden) * scale + shift).astype(BF16)

    copies[0].wait()
    copies[1].wait()

    @pl.loop(0, rows_own // tile)
    def _(t):
        rows, hidden, attn_in = embed(t)
        h_ref[rows, :] = hidden
        kv_s[rows, :] = jnp.dot(attn_in, kv_w[...], preferred_element_type=F32).astype(BF16)
        q = jnp.dot(attn_in, q_w[...], preferred_element_type=F32).astype(BF16)
        q_s[rows, :] = q * BF16(1.0 / math.sqrt(HEAD_DIM))

    @pl.loop(rows_own // tile, seq // tile)
    def _(t):
        rows, _, attn_in = embed(t)
        kv_s[rows, :] = jnp.dot(attn_in, kv_w[...], preferred_element_type=F32).astype(BF16)

    pair = 2 * HEAD_DIM
    first = lax.broadcasted_iota(jnp.int32, (tile, pair), 1) < HEAD_DIM

    @pl.loop(0, width // pair)
    def _(hp):
        cols = pl.ds(pl.multiple_of(hp * pair, pair), pair)
        keys = kv_s[:, cols]
        values = kv_s[:, pl.ds(pl.multiple_of(width + hp * pair, pair), pair)]
        for t in range(rows_own // tile):
            rows = slice(t * tile, (t + 1) * tile)
            q2 = q_s[rows, cols]
            outs = []
            for mask in (first, jnp.logical_not(first)):
                s = lax.dot_general(
                    jnp.where(mask, q2, BF16(0)),
                    keys,
                    (((1,), (1,)), ((), ())),
                    preferred_element_type=F32,
                )
                p = jnp.exp(s - jnp.max(s, axis=-1, keepdims=True))
                total = jnp.sum(p, axis=-1, keepdims=True)
                o = jnp.dot(p.astype(BF16), values, preferred_element_type=F32)
                outs.append(o * (1.0 / total))
            att_s[rows, cols] = jnp.where(first, outs[0], outs[1]).astype(BF16)

    copies[2].wait()

    @pl.loop(0, rows_own // tile)
    def _(t):
        rows = pl.ds(pl.multiple_of(t * tile, tile), tile)
        h_ref[rows, :] += gate * jnp.dot(att_s[rows, :], out_w[...], preferred_element_type=F32)


def mlp_kernel(
    tile,
    block,
    coef_ref,
    x_ref,
    h_ref,
    mod_ref,
    final_ref,
    up_a,
    up_b,
    down_a,
    down_b,
    d_ref,
    up_w,
    down_w,
    sems,
):
    rows_own, width = h_ref.shape
    hidden_units = up_w.shape[2]
    copies = []
    for i, (src, dst) in enumerate(
        ((up_a, up_w.at[0]), (down_a, down_w.at[0]), (up_b, up_w.at[1]), (down_b, down_w.at[1]))
    ):
        copy = pltpu.make_async_copy(src, dst, sems.at[i])
        copy.start()
        copies.append(copy)
    shift, scale, gate = mod_ref[3:4, :], 1.0 + mod_ref[4:5, :], mod_ref[5:6, :]
    shift_o, scale_o = mod_ref[6:7, :], 1.0 + mod_ref[7:8, :]
    for copy in copies:
        copy.wait()

    @pl.loop(0, rows_own // tile)
    def _(t):
        rows = pl.ds(pl.multiple_of(t * tile, tile), tile)
        h = h_ref[rows, :]
        x = (normed(h) * scale + shift).astype(BF16)
        total = jnp.zeros((tile, width), F32)
        for half in range(2):
            acc = jnp.zeros((tile, width), F32)
            for j in range(hidden_units // block):
                part = slice(j * block, (j + 1) * block)
                lifted = jnp.dot(x, up_w[half, :, part], preferred_element_type=F32)
                lifted = jax.nn.gelu(lifted, approximate=True).astype(BF16)
                acc = acc + jnp.dot(lifted, down_w[half, part, :], preferred_element_type=F32)
            total = total + acc.astype(BF16).astype(F32)
        h2 = h + gate * total
        final_in = (normed(h2) * scale_o + shift_o).astype(BF16)
        eps = lax.dot_general(
            final_ref[...], final_in, (((1,), (1,)), ((), ())), preferred_element_type=F32
        )
        d_ref[:, rows] = (coef_ref[0] * x_ref[:, rows] + coef_ref[1] * eps).astype(BF16)


def prefix_kernel(
    count,
    d_ref,
    prev_ref,
    now_ref,
    held,
    other_d,
    mine,
    other_sum,
    send_sem,
    recv_sem,
    pair_send,
    pair_recv,
):
    here = lax.axis_index("tm")
    core = lax.axis_index("tensor")
    partner = (here, 1 - core)

    def to(target):
        return pltpu.make_async_remote_copy(
            src_ref=d_ref,
            dst_ref=held.at[here],
            send_sem=send_sem.at[target],
            recv_sem=recv_sem.at[here],
            device_id=(target, core),
            device_id_type=MESH,
        )

    def across(src, dst, slot):
        return pltpu.make_async_remote_copy(
            src_ref=src,
            dst_ref=dst,
            send_sem=pair_send.at[slot],
            recv_sem=pair_recv.at[slot],
            device_id=partner,
            device_id_type=MESH,
        )

    barrier = pltpu.get_barrier_semaphore()
    pl.semaphore_signal(barrier, inc=1, device_id=partner, device_id_type=MESH)

    @pl.loop(0, here)
    def _(j):
        pl.semaphore_signal(barrier, inc=1, device_id=(j, core), device_id_type=MESH)

    pl.semaphore_wait(barrier, count - here)

    @pl.loop(here + 1, count)
    def _(t):
        to(t).start()

    swap = across(d_ref, other_d, 0)
    swap.start()

    def add(j, total):
        pltpu.make_async_remote_copy(
            src_ref=d_ref,
            dst_ref=held.at[j],
            send_sem=send_sem.at[j],
            recv_sem=recv_sem.at[j],
            device_id=partner,
            device_id_type=MESH,
        ).wait_recv()
        return total + held[j].astype(F32)

    before = lax.fori_loop(0, here, add, jnp.zeros(d_ref.shape, F32))
    mine[...] = before.astype(BF16)
    swap_sum = across(mine, other_sum, 1)
    swap_sum.start()
    prev_ref[0] = before
    now_ref[0] = before + d_ref[...].astype(F32)
    swap.wait()
    swap_sum.wait()
    behind = other_sum[...].astype(F32)
    prev_ref[1] = behind
    now_ref[1] = behind + other_d[...].astype(F32)

    @pl.loop(here + 1, count)
    def _(t):
        to(t).wait_send()


def run_attention(x, patch, tables, mods, q_w, kv_w, out_w, rows_own):
    width = q_w.shape[0]
    seq = x.shape[1]
    tile = 256
    flops = 2 * seq * width * 2 * width + 4 * rows_own * width * width + 16 * rows_own * seq * width
    return pl.pallas_call(
        functools.partial(attention_kernel, tile),
        out_shape=jax.ShapeDtypeStruct((rows_own, width), F32),
        in_specs=[VM] * 7 + [ANY] * 3,
        out_specs=VM,
        scratch_shapes=[
            pltpu.VMEM((seq, 2 * width), BF16),
            pltpu.VMEM((rows_own, width), BF16),
            pltpu.VMEM((rows_own, width), BF16),
            pltpu.VMEM(q_w.shape, BF16),
            pltpu.VMEM(kv_w.shape, BF16),
            pltpu.VMEM(out_w.shape, BF16),
            pltpu.SemaphoreType.DMA((3,)),
        ],
        compiler_params=pltpu.CompilerParams(vmem_limit_bytes=LIMIT),
        cost_estimate=pl.CostEstimate(
            flops=flops, bytes_accessed=8_000_000, transcendentals=rows_own * seq * width // 64
        ),
        name="attention",
    )(x, patch, *tables, mods, q_w, kv_w, out_w)


def run_mlp(coefs, x_own, h, mods, final_t, up_a, up_b, down_a, down_b):
    rows_own, width = h.shape
    units = up_a.shape[1]
    return pl.pallas_call(
        functools.partial(mlp_kernel, 256, 512),
        out_shape=jax.ShapeDtypeStruct((final_t.shape[0], rows_own), BF16),
        in_specs=[SM] + [VM] * 4 + [ANY] * 4,
        out_specs=VM,
        scratch_shapes=[
            pltpu.VMEM((2, width, units), BF16),
            pltpu.VMEM((2, units, width), BF16),
            pltpu.SemaphoreType.DMA((4,)),
        ],
        compiler_params=pltpu.CompilerParams(vmem_limit_bytes=LIMIT),
        cost_estimate=pl.CostEstimate(
            flops=8 * rows_own * width * units, bytes_accessed=12_000_000, transcendentals=0
        ),
        name="feed_forward",
    )(coefs, x_own, h, mods, final_t, up_a, up_b, down_a, down_b)


def run_prefix(count, drift):
    part = drift.shape
    both = jax.ShapeDtypeStruct((2,) + part, F32)
    return pl.pallas_call(
        functools.partial(prefix_kernel, count),
        out_shape=(both, both),
        in_specs=[VM],
        out_specs=(VM, VM),
        scratch_shapes=[
            pltpu.VMEM((count,) + part, BF16),
            pltpu.VMEM(part, BF16),
            pltpu.VMEM(part, BF16),
            pltpu.VMEM(part, BF16),
            pltpu.SemaphoreType.DMA((count,)),
            pltpu.SemaphoreType.DMA((count,)),
            pltpu.SemaphoreType.DMA((2,)),
            pltpu.SemaphoreType.DMA((2,)),
        ],
        compiler_params=pltpu.CompilerParams(collective_id=0, has_side_effects=True),
        name="prefix",
    )(drift)


def per_device(
    noise_start,
    timesteps,
    class_labels,
    mixing,
    class_table,
    time_in,
    time_out,
    ada_weight,
    final_ada,
    patch_weight,
    q_weight,
    kv_weight,
    out_weight,
    up_weight,
    down_weight,
    final_weight,
):
    count = lax.axis_size("tm")
    point = lax.axis_index("tm")
    member = lax.axis_index("tensor")
    patch, width = patch_weight.shape
    seq = noise_start.shape[1] // patch
    rows_own = seq // 2
    swap = [(0, 1), (1, 0)]
    up_other = lax.ppermute(up_weight, "tensor", swap)
    down_other = lax.ppermute(down_weight, "tensor", swap)
    mixing_before = lax.ppermute(mixing, "tm", [(i, i + 1) for i in range(count - 1)])

    moments = jnp.stack([pick_entry(timesteps, point), pick_entry(timesteps, point + 1)])
    alphas = alpha_at(moments)
    keep_coef = jnp.sqrt(alphas[1] / alphas[0])
    noise_coef = jnp.sqrt(1.0 - alphas[1]) - jnp.sqrt(alphas[1] * (1.0 - alphas[0]) / alphas[0])
    coefs = jnp.stack([keep_coef - 1.0, noise_coef])

    features = time_features(moments[0], time_in.shape[0] // 2).astype(BF16)
    time_hidden = jax.nn.silu(jnp.dot(features, time_in, preferred_element_type=F32)).astype(BF16)
    time_embed = jnp.dot(time_hidden, time_out, preferred_element_type=F32)
    classes = lax.dynamic_slice_in_dim(class_table, class_labels[0, 0], 1, 0).astype(F32)
    cond = jax.nn.silu(time_embed + classes).astype(BF16)
    modul = jnp.dot(cond, ada_weight, preferred_element_type=F32)
    final_mod = jnp.dot(cond, final_ada, preferred_element_type=F32)
    mods = jnp.concatenate([modul, final_mod], axis=1).reshape(8, width)

    half_width = width // 2
    rates = jnp.exp(-math.log(10000.0) * jnp.arange(half_width, dtype=F32) / half_width)
    near = jnp.arange(PERIOD, dtype=F32)[:, None] * rates[None]
    spans = seq // PERIOD
    turn = (jnp.arange(spans, dtype=jnp.int32) + member * (spans // 2)) % spans
    far = (turn * PERIOD).astype(F32)[:, None] * rates[None]
    tables = (jnp.sin(far), jnp.cos(far), jnp.sin(near), jnp.cos(near))

    plain = noise_start.reshape(seq, patch).T.reshape(patch, 2, rows_own)
    swapped = plain[:, ::-1]
    noise = jnp.where(member == 0, plain, swapped).reshape(patch, seq)
    halves = jnp.stack([noise[:, :rows_own], noise[:, rows_own:]])
    final_t = final_weight.T

    def denoise(x):
        h = run_attention(
            x, patch_weight, tables, mods, q_weight, kv_weight, out_weight, rows_own
        )
        drift = run_mlp(
            coefs, x[:, :rows_own], h, mods, final_t, up_weight, up_other, down_weight, down_other
        )
        return run_prefix(count, drift)

    before, sums = denoise(noise)
    residuals = [jnp.mean(jnp.square(sums))]
    state = halves + (1.0 + mixing[0, 0]) * sums
    x = halves + (1.0 + mixing_before[0, 0]) * before
    _, sums_next = denoise(jnp.concatenate([x[0], x[1]], axis=1))
    picard = halves + sums_next
    residuals.append(jnp.mean(jnp.square(picard - state)))
    state = picard + mixing[1, 0] * (sums_next - sums)
    ordered = jnp.where(member == 0, state, state[::-1])
    states = ordered.transpose(0, 2, 1).reshape(1, 1, seq * patch)
    return (states, jnp.stack(residuals)[:, None])


def solution(mesh):
    in_specs = (
        P(),
        P(),
        P("tm", None),
        P(None, "tm"),
        P(),
        P(),
        P(),
        P(),
        P(),
        P(),
        P(),
        P(),
        P(),
        P(None, "tensor"),
        P("tensor", None),
        P(),
    )
    out_specs = (P("tm", None, None), P(None, "tm"))
    return jax.shard_map(
        per_device, mesh=mesh, in_specs=in_specs, out_specs=out_specs, check_vma=False
    )
```

```python
import functools
import math

import jax
import jax.numpy as jnp
from jax import lax
from jax.experimental import pallas as pl
from jax.experimental.pallas import tpu as pltpu
from jax.sharding import PartitionSpec as P
import numpy as np

HEAD_DIM = 64
ITERS = 2
PERIOD = 32
norm_eps = 1e-06
plan_steps = 1000
MESH = pl.DeviceIdType.MESH
F32 = jnp.float32
BF16 = jnp.bfloat16
ANY = pl.BlockSpec(memory_space=pl.ANY)
VM = pl.BlockSpec(memory_space=pltpu.VMEM)
SM = pl.BlockSpec(memory_space=pltpu.SMEM)
LIMIT = 56 * 1024 * 1024


def normed(values):
    center = values - jnp.mean(values, axis=-1, keepdims=True)
    spread = jnp.mean(center * center, axis=-1, keepdims=True)
    return center * lax.rsqrt(spread + norm_eps)


def attention_kernel(
    tile,
    x_ref,
    patch_ref,
    far_sin,
    far_cos,
    near_sin,
    near_cos,
    mod_ref,
    q_hbm,
    kv_hbm,
    out_hbm,
    h_ref,
    kv_s,
    q_s,
    att_s,
    q_w,
    kv_w,
    out_w,
    sems,
):
    rows_own, width = h_ref.shape
    seq = x_ref.shape[1]
    copies = [
        pltpu.make_async_copy(src, dst, sems.at[i])
        for i, (src, dst) in enumerate(((kv_hbm, kv_w), (q_hbm, q_w), (out_hbm, out_w)))
    ]
    for copy in copies:
        copy.start()
    shift, scale, gate = mod_ref[0:1, :], 1.0 + mod_ref[1:2, :], mod_ref[2:3, :]
    groups = tile // PERIOD
    spans = far_sin.shape[0]
    member = lax.axis_index("tensor")

    def embed(t):
        rows = pl.ds(pl.multiple_of(t * tile, tile), tile)
        tokens = x_ref[:, rows].astype(BF16)
        hidden = lax.dot_general(
            tokens, patch_ref[...], (((0,), (0,)), ((), ())), preferred_element_type=F32
        )
        turn = lax.rem(t * groups + member * (spans // 2), spans)
        far = pl.ds(pl.multiple_of(turn, groups), groups)
        fs, fc = far_sin[far, :][:, None, :], far_cos[far, :][:, None, :]
        ns, nc = near_sin[...][None], near_cos[...][None]
        sines = (fs * nc + fc * ns).reshape(tile, width // 2)
        cosines = (fc * nc - fs * ns).reshape(tile, width // 2)
        hidden = hidden + jnp.concatenate([sines, cosines], axis=1)
        return rows, hidden, (normed(hidden) * scale + shift).astype(BF16)

    copies[0].wait()
    copies[1].wait()

    @pl.loop(0, rows_own // tile)
    def _(t):
        rows, hidden, attn_in = embed(t)
        h_ref[rows, :] = hidden
        kv_s[rows, :] = jnp.dot(attn_in, kv_w[...], preferred_element_type=F32).astype(BF16)
        q = jnp.dot(attn_in, q_w[...], preferred_element_type=F32).astype(BF16)
        q_s[rows, :] = q * BF16(1.0 / math.sqrt(HEAD_DIM))

    @pl.loop(rows_own // tile, seq // tile)
    def _(t):
        rows, _, attn_in = embed(t)
        kv_s[rows, :] = jnp.dot(attn_in, kv_w[...], preferred_element_type=F32).astype(BF16)

    pair = 2 * HEAD_DIM
    first = lax.broadcasted_iota(jnp.int32, (tile, pair), 1) < HEAD_DIM

    @pl.loop(0, width // pair)
    def _(hp):
        cols = pl.ds(pl.multiple_of(hp * pair, pair), pair)
        keys = kv_s[:, cols]
        values = kv_s[:, pl.ds(pl.multiple_of(width + hp * pair, pair), pair)]
        for t in range(rows_own // tile):
            rows = slice(t * tile, (t + 1) * tile)
            q2 = q_s[rows, cols]
            outs = []
            for mask in (first, jnp.logical_not(first)):
                s = lax.dot_general(
                    jnp.where(mask, q2, BF16(0)),
                    keys,
                    (((1,), (1,)), ((), ())),
                    preferred_element_type=F32,
                )
                p = jnp.exp(s - jnp.max(s, axis=-1, keepdims=True))
                total = jnp.sum(p, axis=-1, keepdims=True)
                o = jnp.dot(p.astype(BF16), values, preferred_element_type=F32)
                outs.append(o * (1.0 / total))
            att_s[rows, cols] = jnp.where(first, outs[0], outs[1]).astype(BF16)

    copies[2].wait()

    @pl.loop(0, rows_own // tile)
    def _(t):
        rows = pl.ds(pl.multiple_of(t * tile, tile), tile)
        h_ref[rows, :] += gate * jnp.dot(att_s[rows, :], out_w[...], preferred_element_type=F32)


def mlp_kernel(
    tile,
    block,
    coef_ref,
    x_ref,
    h_ref,
    mod_ref,
    final_ref,
    up_a,
    up_b,
    down_a,
    down_b,
    d_ref,
    in_s,
    sum_s,
    up_w,
    down_w,
    sems,
):
    rows_own, width = h_ref.shape
    hidden_units = up_w.shape[2]
    copies = []
    for i, (src, dst) in enumerate(
        ((up_a, up_w.at[0]), (down_a, down_w.at[0]), (up_b, up_w.at[1]), (down_b, down_w.at[1]))
    ):
        copy = pltpu.make_async_copy(src, dst, sems.at[i])
        copy.start()
        copies.append(copy)
    shift, scale, gate = mod_ref[3:4, :], 1.0 + mod_ref[4:5, :], mod_ref[5:6, :]
    shift_o, scale_o = mod_ref[6:7, :], 1.0 + mod_ref[7:8, :]
    keep, noise = coef_ref[0:1, 0:1], coef_ref[1:2, 0:1]
    tiles = rows_own // tile

    def rows_of(t):
        return pl.ds(pl.multiple_of(t * tile, tile), tile)

    @pl.loop(0, tiles)
    def _(t):
        in_s[rows_of(t), :] = (normed(h_ref[rows_of(t), :]) * scale + shift).astype(BF16)

    for half in range(2):
        copies[2 * half].wait()
        copies[2 * half + 1].wait()

        @pl.loop(0, tiles)
        def _(t):
            rows = rows_of(t)
            x = in_s[rows, :]
            acc = jnp.zeros((tile, width), F32)
            for j in range(hidden_units // block):
                part = slice(j * block, (j + 1) * block)
                lifted = jnp.dot(x, up_w[half, :, part], preferred_element_type=F32)
                lifted = jax.nn.gelu(lifted, approximate=True).astype(BF16)
                acc = acc + jnp.dot(lifted, down_w[half, part, :], preferred_element_type=F32)
            acc = acc.astype(BF16).astype(F32)
            if half == 0:
                sum_s[rows, :] = acc
            else:
                h2 = h_ref[rows, :] + gate * (sum_s[rows, :] + acc)
                final_in = (normed(h2) * scale_o + shift_o).astype(BF16)
                eps = lax.dot_general(
                    final_ref[...], final_in, (((1,), (1,)), ((), ())), preferred_element_type=F32
                )
                d_ref[:, rows] = (keep * x_ref[:, rows] + noise * eps).astype(BF16)


def setup_kernel(
    times_ref,
    label_ref,
    noise_ref,
    mixing_ref,
    table_hbm,
    in_hbm,
    out_hbm,
    ada_hbm,
    final_hbm,
    mod_ref,
    coef_ref,
    mix_ref,
    halves_ref,
    x_ref,
    rows_v,
    in_v,
    out_v,
    ada_v,
    final_v,
    sems,
):
    here = lax.axis_index("tm")
    member = lax.axis_index("tensor")
    label = label_ref[0, 0]
    width = mod_ref.shape[1]
    base = pl.multiple_of(label // 8 * 8, 8)
    copies = []

    def begin(src, dst):
        copy = pltpu.make_async_copy(src, dst, sems.at[len(copies)])
        copy.start()
        copies.append(copy)

    begin(in_hbm, in_v)
    begin(out_hbm, out_v)
    begin(table_hbm.at[pl.ds(base, 8), :], rows_v)
    parts = []
    for src, dst in ((ada_hbm, ada_v), (final_hbm, final_v)):
        for j in range(src.shape[1] // width):
            cols = slice(j * width, (j + 1) * width)
            begin(src.at[:, cols], dst.at[:, cols])
            parts.append(dst.at[:, cols])

    level = lax.broadcasted_iota(jnp.int32, (8, 128), 0) * 128
    level = level + lax.broadcasted_iota(jnp.int32, (8, 128), 1)
    beta = 0.0001 + (0.02 - 0.0001) * level.astype(F32) / (plan_steps - 1)
    logs = jnp.log(1.0 - beta)
    now = times_ref[here]

    def alpha(moment):
        kept = jnp.where(level <= moment, logs, 0.0)
        total = jnp.sum(jnp.sum(kept, axis=1, keepdims=True), axis=0, keepdims=True)
        return jnp.exp(total)

    before, after = alpha(now), alpha(times_ref[here + 1])
    keep = jnp.sqrt(after / before) - 1.0
    noise = jnp.sqrt(1.0 - after) - jnp.sqrt(after * (1.0 - before) / before)
    coef_ref[0:1, :] = jnp.broadcast_to(keep, (1, 128))
    coef_ref[1:2, :] = jnp.broadcast_to(noise, (1, 128))
    coef_ref[2:8, :] = jnp.zeros((6, 128), F32)
    mix_ref[0:2, :] = jnp.broadcast_to(mixing_ref[...], (2, 128))
    mix_ref[2:8, :] = jnp.zeros((6, 128), F32)

    plain = noise_ref[...]
    half = plain.shape[1] // 2
    left, right = plain[:, :half], plain[:, half:]
    first = member == 0
    own, other = jnp.where(first, left, right), jnp.where(first, right, left)
    halves_ref[0] = own
    halves_ref[1] = other
    x_ref[:, :half] = own
    x_ref[:, half:] = other

    count = in_v.shape[0] // 2
    lane = lax.broadcasted_iota(jnp.int32, (8, count), 1).astype(F32)
    angle = now.astype(F32) * jnp.exp(-math.log(10000.0) * lane / count)
    features = jnp.concatenate([jnp.cos(angle), jnp.sin(angle)], axis=1).astype(BF16)
    copies[0].wait()
    hidden = jax.nn.silu(jnp.dot(features, in_v[...], preferred_element_type=F32)).astype(BF16)
    copies[1].wait()
    embed = jnp.dot(hidden, out_v[...], preferred_element_type=F32)
    copies[2].wait()
    picked = lax.broadcasted_iota(jnp.int32, (8, width), 0) == label - base
    entry = jnp.sum(jnp.where(picked, rows_v[...].astype(F32), 0.0), axis=0, keepdims=True)
    cond = jax.nn.silu(embed + entry).astype(BF16)
    for j, part in enumerate(parts):
        copies[3 + j].wait()
        mod_ref[j : j + 1, :] = jnp.dot(cond, part[...], preferred_element_type=F32)[0:1, :]


def prefix_kernel(
    count,
    inner,
    last,
    d_ref,
    noise_ref,
    mix_ref,
    *rest,
):
    if last:
        sums_in, state_ref, res_ref, *rest = rest
    else:
        sums_out, x_ref, res_ref, *rest = rest
    held, totals, mine, mix_in, send_a, recv_a, send_b, recv_b, send_m, recv_m = rest
    here = lax.axis_index("tm")
    core = lax.axis_index("tensor")
    outer = count // inner
    group, place = here // inner, here % inner
    start = group * inner

    def copy(src, dst, send, recv, target, target_core):
        return pltpu.make_async_remote_copy(
            src_ref=src,
            dst_ref=dst,
            send_sem=send,
            recv_sem=recv,
            device_id=(target, target_core),
            device_id_type=MESH,
        )

    def inside(i, c):
        return copy(
            d_ref, held.at[place, core], send_a.at[i, c], recv_a.at[place, core], start + i, c
        )

    def onward(g, c):
        return copy(
            mine,
            totals.at[group, core],
            send_b.at[g, c],
            recv_b.at[group, core],
            g * inner + place,
            c,
        )

    def neighbour():
        return copy(mix_ref, mix_in, send_m.at[0], recv_m.at[0], here + 1, core)

    barrier = pltpu.get_barrier_semaphore()

    def greet(target, c):
        pl.semaphore_signal(barrier, inc=1, device_id=(target, c), device_id_type=MESH)

    def others(act):
        act(place, 1 - core)

        @pl.loop(1, inner)
        def _(step):
            i = lax.rem(place + step, inner)
            act(i, 0)
            act(i, 1)

    others(lambda i, c: greet(start + i, c))

    @pl.loop(0, group)
    def _(g):
        greet(g * inner + place, 0)
        greet(g * inner + place, 1)

    waits = 2 * inner - 1 + 2 * (outer - 1 - group)
    if not last:

        @pl.when(here > 0)
        def _():
            greet(here - 1, core)

        waits = waits + jnp.where(here < count - 1, 1, 0)
    pl.semaphore_wait(barrier, waits)

    others(lambda i, c: inside(i, c).start())
    if not last:

        @pl.when(here < count - 1)
        def _():
            neighbour().start()

        @pl.when(here == 0)
        def _():
            mix_in[...] = jnp.zeros_like(mix_in)

    held[place, core] = d_ref[...]

    def arrive_inside(i, c):
        copy(
            d_ref, held.at[i, c], send_a.at[i, c], recv_a.at[i, c], start + i, c
        ).wait_recv()

    others(arrive_inside)
    total = jnp.zeros(d_ref.shape, F32)
    for i in range(inner):
        total = total + held[i, core].astype(F32)
    mine[...] = total.astype(BF16)

    @pl.loop(group + 1, outer)
    def _(g):
        onward(g, 0).start()
        onward(g, 1).start()

    def partial(c):
        def add(i, acc):
            return acc + held[i, c].astype(F32)

        return lax.fori_loop(0, place, add, jnp.zeros(d_ref.shape, F32))

    before = [partial(core), partial(1 - core)]

    @pl.loop(0, group)
    def _(g):
        for c in range(2):
            copy(
                mine,
                totals.at[g, c],
                send_b.at[g, c],
                recv_b.at[g, c],
                g * inner + place,
                c,
            ).wait_recv()

    def gather(c, acc):
        return lax.fori_loop(0, group, lambda g, a: a + totals[g, c].astype(F32), acc)

    before = [gather(core, before[0]), gather(1 - core, before[1])]
    own = held[place, core].astype(F32)
    other = held[place, 1 - core].astype(F32)
    sums = [before[0] + own, before[1] + other]
    noise = [noise_ref[0], noise_ref[1]]
    half = d_ref.shape[1]
    scale = 1.0 / (2 * d_ref.shape[0] * half)

    def mean_square(values):
        total = sum(v * v for v in values)
        total = jnp.sum(jnp.sum(total, axis=1, keepdims=True), axis=0, keepdims=True)
        return jnp.broadcast_to(total * scale, res_ref.shape)

    mix = mix_ref[0:1, 0:1]
    if last:
        old = [sums_in[0], sums_in[1]]
        state = [n + (1.0 + mix) * o for n, o in zip(noise, old)]
        picard = [n + s for n, s in zip(noise, sums)]
        res_ref[...] = mean_square([g - s for g, s in zip(picard, state)])
        mix = mix_ref[1:2, 0:1]
        new = [g + mix * (s - o) for g, s, o in zip(picard, sums, old)]
        first = core == 0
        state_ref[:, :half] = jnp.where(first, new[0], new[1])
        state_ref[:, half:] = jnp.where(first, new[1], new[0])
    else:
        sums_out[0] = sums[0]
        sums_out[1] = sums[1]
        res_ref[...] = mean_square(sums)

        @pl.when(here > 0)
        def _():
            copy(mix_ref, mix_in, send_m.at[0], recv_m.at[0], here - 1, core).wait_recv()

        mix = 1.0 + mix_in[0:1, 0:1]
        x_ref[:, :half] = noise[0] + mix * before[0]
        x_ref[:, half:] = noise[1] + mix * before[1]

        @pl.when(here < count - 1)
        def _():
            neighbour().wait_send()

    others(lambda i, c: inside(i, c).wait_send())

    @pl.loop(group + 1, outer)
    def _(g):
        onward(g, 0).wait_send()
        onward(g, 1).wait_send()


def run_attention(x, patch, tables, mods, q_w, kv_w, out_w, rows_own):
    width = q_w.shape[0]
    seq = x.shape[1]
    tile = 256
    flops = 2 * seq * width * 2 * width + 4 * rows_own * width * width + 16 * rows_own * seq * width
    return pl.pallas_call(
        functools.partial(attention_kernel, tile),
        out_shape=jax.ShapeDtypeStruct((rows_own, width), F32),
        in_specs=[VM] * 7 + [ANY] * 3,
        out_specs=VM,
        scratch_shapes=[
            pltpu.VMEM((seq, 2 * width), BF16),
            pltpu.VMEM((rows_own, width), BF16),
            pltpu.VMEM((rows_own, width), BF16),
            pltpu.VMEM(q_w.shape, BF16),
            pltpu.VMEM(kv_w.shape, BF16),
            pltpu.VMEM(out_w.shape, BF16),
            pltpu.SemaphoreType.DMA((3,)),
        ],
        compiler_params=pltpu.CompilerParams(vmem_limit_bytes=LIMIT),
        cost_estimate=pl.CostEstimate(
            flops=flops, bytes_accessed=8_000_000, transcendentals=rows_own * seq * width // 64
        ),
        name="attention",
    )(x, patch, *tables, mods, q_w, kv_w, out_w)


def run_mlp(coefs, x_own, h, mods, final_t, up_a, up_b, down_a, down_b):
    rows_own, width = h.shape
    units = up_a.shape[1]
    return pl.pallas_call(
        functools.partial(mlp_kernel, 256, 512),
        out_shape=jax.ShapeDtypeStruct((final_t.shape[0], rows_own), BF16),
        in_specs=[VM] * 5 + [ANY] * 4,
        out_specs=VM,
        scratch_shapes=[
            pltpu.VMEM((rows_own, width), BF16),
            pltpu.VMEM((rows_own, width), F32),
            pltpu.VMEM((2, width, units), BF16),
            pltpu.VMEM((2, units, width), BF16),
            pltpu.SemaphoreType.DMA((4,)),
        ],
        compiler_params=pltpu.CompilerParams(vmem_limit_bytes=LIMIT),
        cost_estimate=pl.CostEstimate(
            flops=8 * rows_own * width * units, bytes_accessed=12_000_000, transcendentals=0
        ),
        name="feed_forward",
    )(coefs, x_own, h, mods, final_t, up_a, up_b, down_a, down_b)


def run_prefix(count, drift, noise, mix, sums=None):
    part = drift.shape
    inner = 1
    while inner * inner < count:
        inner *= 2
    last = sums is not None
    both = jax.ShapeDtypeStruct((2,) + part, F32)
    flat = jax.ShapeDtypeStruct((part[0], 2 * part[1]), F32)
    small = jax.ShapeDtypeStruct((8, 128), F32)
    return pl.pallas_call(
        functools.partial(prefix_kernel, count, inner, last),
        out_shape=(flat, small) if last else (both, flat, small),
        in_specs=[VM] * (4 if last else 3),
        out_specs=(VM,) * (2 if last else 3),
        scratch_shapes=[
            pltpu.VMEM((inner, 2) + part, BF16),
            pltpu.VMEM((count // inner, 2) + part, BF16),
            pltpu.VMEM(part, BF16),
            pltpu.VMEM((8, 128), F32),
            pltpu.SemaphoreType.DMA((inner, 2)),
            pltpu.SemaphoreType.DMA((inner, 2)),
            pltpu.SemaphoreType.DMA((count // inner, 2)),
            pltpu.SemaphoreType.DMA((count // inner, 2)),
            pltpu.SemaphoreType.DMA((1,)),
            pltpu.SemaphoreType.DMA((1,)),
        ],
        compiler_params=pltpu.CompilerParams(
            collective_id=1 if last else 0, has_side_effects=True
        ),
        name="prefix_last" if last else "prefix",
    )(drift, noise, mix, *((sums,) if last else ()))


def run_setup(times, label, noise, mixing, table, time_in, time_out, ada, final_ada):
    patch, seq = noise.shape
    width = time_out.shape[0]
    small = jax.ShapeDtypeStruct((8, 128), F32)
    return pl.pallas_call(
        setup_kernel,
        out_shape=(
            jax.ShapeDtypeStruct((8, width), F32),
            small,
            small,
            jax.ShapeDtypeStruct((2, patch, seq // 2), F32),
            jax.ShapeDtypeStruct((patch, seq), F32),
        ),
        in_specs=[SM, SM, VM, VM] + [ANY] * 5,
        out_specs=(VM,) * 5,
        scratch_shapes=[
            pltpu.VMEM((8, width), BF16),
            pltpu.VMEM(time_in.shape, BF16),
            pltpu.VMEM(time_out.shape, BF16),
            pltpu.VMEM(ada.shape, BF16),
            pltpu.VMEM(final_ada.shape, BF16),
            pltpu.SemaphoreType.DMA((11,)),
        ],
        compiler_params=pltpu.CompilerParams(vmem_limit_bytes=LIMIT),
        cost_estimate=pl.CostEstimate(flops=0, bytes_accessed=12_000_000, transcendentals=0),
        name="setup",
    )(times, label, noise, mixing, table, time_in, time_out, ada, final_ada)


def per_device(
    noise_start,
    timesteps,
    class_labels,
    mixing,
    class_table,
    time_in,
    time_out,
    ada_weight,
    final_ada,
    patch_weight,
    q_weight,
    kv_weight,
    out_weight,
    up_weight,
    down_weight,
    final_weight,
):
    count = lax.axis_size("tm")
    patch, width = patch_weight.shape
    seq = noise_start.shape[1] // patch
    rows_own = seq // 2
    swap = [(0, 1), (1, 0)]
    up_other = lax.ppermute(up_weight, "tensor", swap)
    down_other = lax.ppermute(down_weight, "tensor", swap)

    plain = noise_start.reshape(seq, patch).T
    mods, coefs, mix, noise, x = run_setup(
        timesteps, class_labels, plain, mixing, class_table, time_in, time_out, ada_weight, final_ada
    )

    half_width = width // 2
    rates = np.exp(-math.log(10000.0) * np.arange(half_width) / half_width)
    near = np.arange(PERIOD)[:, None] * rates[None]
    far = np.arange(seq // PERIOD)[:, None] * PERIOD * rates[None]
    tables = [
        jnp.asarray(t.astype(np.float32))
        for t in (np.sin(far), np.cos(far), np.sin(near), np.cos(near))
    ]
    final_t = final_weight.T

    def drift_of(x):
        h = run_attention(
            x, patch_weight, tables, mods, q_weight, kv_weight, out_weight, rows_own
        )
        return run_mlp(coefs, x, h, mods, final_t, up_weight, up_other, down_weight, down_other)

    sums, x, first = run_prefix(count, drift_of(x), noise, mix)
    state, second = run_prefix(count, drift_of(x), noise, mix, sums)
    states = state.T.reshape(1, 1, seq * patch)
    return (states, jnp.stack([first[0, 0], second[0, 0]])[:, None])


def solution(mesh):
    in_specs = (
        P(),
        P(),
        P("tm", None),
        P(None, "tm"),
        P(),
        P(),
        P(),
        P(),
        P(),
        P(),
        P(),
        P(),
        P(),
        P(None, "tensor"),
        P("tensor", None),
        P(),
    )
    out_specs = (P("tm", None, None), P(None, "tm"))
    return jax.shard_map(
        per_device, mesh=mesh, in_specs=in_specs, out_specs=out_specs, check_vma=False
    )
```

```python
import functools
import math

import jax
import jax.numpy as jnp
from jax import lax
from jax.experimental import pallas as pl
from jax.experimental.pallas import tpu as pltpu
from jax.sharding import PartitionSpec as P
import numpy as np

HEAD_DIM = 64
ITERS = 2
LANES = 128
norm_eps = 1e-06
plan_steps = 1000
MESH = pl.DeviceIdType.MESH
F32 = jnp.float32
BF16 = jnp.bfloat16
ANY = pl.BlockSpec(memory_space=pl.ANY)
VM = pl.BlockSpec(memory_space=pltpu.VMEM)
SM = pl.BlockSpec(memory_space=pltpu.SMEM)
LIMIT = 56 * 1024 * 1024


def normed(values):
    center = values - jnp.mean(values, axis=-1, keepdims=True)
    spread = jnp.mean(center * center, axis=-1, keepdims=True)
    return center * lax.rsqrt(spread + norm_eps)


def attention_kernel(
    tile,
    x_ref,
    patch_ref,
    far_sin,
    far_cos,
    near_sin,
    near_cos,
    mod_ref,
    q_hbm,
    kv_hbm,
    out_hbm,
    h_ref,
    in_s,
    kv_s,
    q_s,
    att_s,
    value_s,
    q_w,
    kv_w,
    out_w,
    sems,
):
    rows_own, width = h_ref.shape
    seq = x_ref.shape[1]
    copies = [
        pltpu.make_async_copy(src, dst, sems.at[i])
        for i, (src, dst) in enumerate(((kv_hbm, kv_w), (q_hbm, q_w), (out_hbm, out_w)))
    ]
    for copy in copies:
        copy.start()
    shift, scale, gate = mod_ref[0:1, :], 1.0 + mod_ref[1:2, :], mod_ref[2:3, :]
    lines = far_sin.shape[0]
    spans = seq // lines
    member = lax.axis_index("tensor")
    fs, fc = far_sin[...], far_cos[...]

    def embed(t):
        rows = slice(t * tile, (t + 1) * tile)
        hidden = lax.dot_general(
            x_ref[:, rows].astype(BF16),
            patch_ref[...],
            (((0,), (0,)), ((), ())),
            preferred_element_type=F32,
        )
        blocks = []
        for i in range(tile // lines):
            turn = lax.rem(t * (tile // lines) + i + member * (spans // 2), spans)
            ns, nc = near_sin[pl.ds(turn, 1), :], near_cos[pl.ds(turn, 1), :]
            blocks.append(jnp.concatenate([fs * nc + fc * ns, fc * nc - fs * ns], axis=1))
        hidden = hidden + jnp.concatenate(blocks, axis=0)
        if t * tile < rows_own:
            h_ref[rows, :] = hidden
        in_s[rows, :] = (normed(hidden) * scale + shift).astype(BF16)

    def project(t):
        rows = slice(t * tile, (t + 1) * tile)
        attn_in = in_s[rows, :]
        kv_s[rows, :] = jnp.dot(attn_in, kv_w[...], preferred_element_type=F32).astype(BF16)
        if t * tile < rows_own:
            q = jnp.dot(attn_in, q_w[...], preferred_element_type=F32).astype(BF16)
            q_s[rows, :] = q * BF16(1.0 / math.sqrt(HEAD_DIM))

    pair = 2 * HEAD_DIM
    value_s[:, pair:] = jnp.ones((seq, pair), BF16)
    embed(0)
    copies[0].wait()
    copies[1].wait()
    for t in range(seq // tile):
        if (t + 1) * tile < seq:
            embed(t + 1)
        project(t)

    first = lax.broadcasted_iota(jnp.int32, (tile, pair), 1) < HEAD_DIM

    @pl.loop(0, width // pair)
    def _(hp):
        cols = pl.ds(pl.multiple_of(hp * pair, pair), pair)
        keys = kv_s[:, cols]
        value_s[:, :pair] = kv_s[:, pl.ds(pl.multiple_of(width + hp * pair, pair), pair)]
        values = value_s[...]
        for t in range(rows_own // tile):
            rows = slice(t * tile, (t + 1) * tile)
            q2 = q_s[rows, cols]
            outs = []
            for mask in (first, jnp.logical_not(first)):
                s = lax.dot_general(
                    jnp.where(mask, q2, BF16(0)),
                    keys,
                    (((1,), (1,)), ((), ())),
                    preferred_element_type=F32,
                )
                p = jnp.exp(s - jnp.max(s, axis=-1, keepdims=True)).astype(BF16)
                o = jnp.dot(p, values, preferred_element_type=F32)
                outs.append(o[:, :pair] / o[:, pair:])
            att_s[rows, cols] = jnp.where(first, outs[0], outs[1]).astype(BF16)

    copies[2].wait()

    @pl.loop(0, rows_own // tile)
    def _(t):
        rows = pl.ds(pl.multiple_of(t * tile, tile), tile)
        h_ref[rows, :] += gate * jnp.dot(att_s[rows, :], out_w[...], preferred_element_type=F32)


def mlp_kernel(
    tile,
    block,
    coef_ref,
    x_ref,
    h_ref,
    mod_ref,
    final_ref,
    up_a,
    up_b,
    down_a,
    down_b,
    d_ref,
    in_s,
    sum_s,
    up_w,
    down_w,
    sems,
):
    rows_own, width = h_ref.shape
    hidden_units = up_w.shape[2]
    copies = []
    for i, (src, dst) in enumerate(
        ((up_a, up_w.at[0]), (down_a, down_w.at[0]), (up_b, up_w.at[1]), (down_b, down_w.at[1]))
    ):
        copy = pltpu.make_async_copy(src, dst, sems.at[i])
        copy.start()
        copies.append(copy)
    shift, scale, gate = mod_ref[3:4, :], 1.0 + mod_ref[4:5, :], mod_ref[5:6, :]
    shift_o, scale_o = mod_ref[6:7, :], 1.0 + mod_ref[7:8, :]
    keep, noise = coef_ref[0:1, 0:1], coef_ref[1:2, 0:1]
    tiles = rows_own // tile

    def rows_of(t):
        return pl.ds(pl.multiple_of(t * tile, tile), tile)

    @pl.loop(0, tiles)
    def _(t):
        in_s[rows_of(t), :] = (normed(h_ref[rows_of(t), :]) * scale + shift).astype(BF16)

    for half in range(2):
        copies[2 * half].wait()
        copies[2 * half + 1].wait()

        @pl.loop(0, tiles)
        def _(t):
            rows = rows_of(t)
            x = in_s[rows, :]
            acc = jnp.zeros((tile, width), F32)
            for j in range(hidden_units // block):
                part = slice(j * block, (j + 1) * block)
                lifted = jnp.dot(x, up_w[half, :, part], preferred_element_type=F32)
                lifted = jax.nn.gelu(lifted, approximate=True).astype(BF16)
                acc = acc + jnp.dot(lifted, down_w[half, part, :], preferred_element_type=F32)
            acc = acc.astype(BF16).astype(F32)
            if half == 0:
                sum_s[rows, :] = acc
            else:
                h2 = h_ref[rows, :] + gate * (sum_s[rows, :] + acc)
                final_in = (normed(h2) * scale_o + shift_o).astype(BF16)
                eps = lax.dot_general(
                    final_ref[...], final_in, (((1,), (1,)), ((), ())), preferred_element_type=F32
                )
                d_ref[:, rows] = (keep * x_ref[:, rows] + noise * eps).astype(BF16)


def setup_kernel(
    times_ref,
    label_ref,
    noise_ref,
    mixing_ref,
    table_hbm,
    in_hbm,
    out_hbm,
    ada_hbm,
    final_hbm,
    mod_ref,
    coef_ref,
    mix_ref,
    halves_ref,
    x_ref,
    rows_v,
    in_v,
    out_v,
    ada_v,
    final_v,
    sems,
):
    here = lax.axis_index("tm")
    member = lax.axis_index("tensor")
    label = label_ref[0, 0]
    width = mod_ref.shape[1]
    base = pl.multiple_of(label // 8 * 8, 8)
    copies = []

    def begin(src, dst):
        copy = pltpu.make_async_copy(src, dst, sems.at[len(copies)])
        copy.start()
        copies.append(copy)

    begin(in_hbm, in_v)
    begin(out_hbm, out_v)
    begin(table_hbm.at[pl.ds(base, 8), :], rows_v)
    parts = []
    for src, dst in ((ada_hbm, ada_v), (final_hbm, final_v)):
        for j in range(src.shape[1] // width):
            cols = slice(j * width, (j + 1) * width)
            begin(src.at[:, cols], dst.at[:, cols])
            parts.append(dst.at[:, cols])

    level = lax.broadcasted_iota(jnp.int32, (8, 128), 0) * 128
    level = level + lax.broadcasted_iota(jnp.int32, (8, 128), 1)
    beta = 0.0001 + (0.02 - 0.0001) * level.astype(F32) / (plan_steps - 1)
    logs = jnp.log(1.0 - beta)
    now = times_ref[here]

    def alpha(moment):
        kept = jnp.where(level <= moment, logs, 0.0)
        total = jnp.sum(jnp.sum(kept, axis=1, keepdims=True), axis=0, keepdims=True)
        return jnp.exp(total)

    before, after = alpha(now), alpha(times_ref[here + 1])
    keep = jnp.sqrt(after / before) - 1.0
    noise = jnp.sqrt(1.0 - after) - jnp.sqrt(after * (1.0 - before) / before)
    coef_ref[0:1, :] = jnp.broadcast_to(keep, (1, 128))
    coef_ref[1:2, :] = jnp.broadcast_to(noise, (1, 128))
    coef_ref[2:8, :] = jnp.zeros((6, 128), F32)
    mix_ref[0:1, :] = jnp.full((1, 128), mixing_ref[0, 0], F32)
    mix_ref[1:2, :] = jnp.full((1, 128), mixing_ref[0, 1], F32)
    mix_ref[2:8, :] = jnp.zeros((6, 128), F32)

    turned = noise_ref[...].T
    patch = x_ref.shape[0]
    blocks = turned.shape[0] // patch // 2
    low = [turned[i * patch : (i + 1) * patch] for i in range(blocks)]
    high = [turned[(blocks + i) * patch : (blocks + i + 1) * patch] for i in range(blocks)]
    left, right = jnp.concatenate(low, axis=1), jnp.concatenate(high, axis=1)
    half = left.shape[1]
    first = member == 0
    own, other = jnp.where(first, left, right), jnp.where(first, right, left)
    halves_ref[0] = own
    halves_ref[1] = other
    x_ref[:, :half] = own
    x_ref[:, half:] = other

    count = in_v.shape[0] // 2
    lane = lax.broadcasted_iota(jnp.int32, (8, count), 1).astype(F32)
    angle = now.astype(F32) * jnp.exp(-math.log(10000.0) * lane / count)
    features = jnp.concatenate([jnp.cos(angle), jnp.sin(angle)], axis=1).astype(BF16)
    copies[0].wait()
    hidden = jax.nn.silu(jnp.dot(features, in_v[...], preferred_element_type=F32)).astype(BF16)
    copies[1].wait()
    embed = jnp.dot(hidden, out_v[...], preferred_element_type=F32)
    copies[2].wait()
    picked = lax.broadcasted_iota(jnp.int32, (8, width), 0) == label - base
    entry = jnp.sum(jnp.where(picked, rows_v[...].astype(F32), 0.0), axis=0, keepdims=True)
    cond = jax.nn.silu(embed + entry).astype(BF16)
    for j, part in enumerate(parts):
        copies[3 + j].wait()
        mod_ref[j : j + 1, :] = jnp.dot(cond, part[...], preferred_element_type=F32)[0:1, :]


def prefix_kernel(
    count,
    inner,
    last,
    d_ref,
    noise_ref,
    mix_ref,
    *rest,
):
    if last:
        sums_in, res_in, state_ref, res_ref, *rest = rest
    else:
        sums_out, x_ref, res_ref, *rest = rest
    held, totals, mine, mix_in, send_a, recv_a, send_b, recv_b, send_m, recv_m = rest
    here = lax.axis_index("tm")
    core = lax.axis_index("tensor")
    outer = count // inner
    group, place = here // inner, here % inner
    start = group * inner

    def copy(src, dst, send, recv, target, target_core):
        return pltpu.make_async_remote_copy(
            src_ref=src,
            dst_ref=dst,
            send_sem=send,
            recv_sem=recv,
            device_id=(target, target_core),
            device_id_type=MESH,
        )

    def inside(i, c):
        return copy(
            d_ref, held.at[place, core], send_a.at[i, c], recv_a.at[place, core], start + i, c
        )

    def onward(g, c):
        return copy(
            mine,
            totals.at[group, core],
            send_b.at[g, c],
            recv_b.at[group, core],
            g * inner + place,
            c,
        )

    def neighbour():
        return copy(mix_ref, mix_in, send_m.at[0], recv_m.at[0], here + 1, core)

    barrier = pltpu.get_barrier_semaphore()

    def greet(target, c):
        pl.semaphore_signal(barrier, inc=1, device_id=(target, c), device_id_type=MESH)

    def others(act):
        act(place, 1 - core)

        @pl.loop(1, inner)
        def _(step):
            i = lax.rem(place + step, inner)
            act(i, 0)
            act(i, 1)

    others(lambda i, c: greet(start + i, c))

    @pl.loop(0, group)
    def _(g):
        greet(g * inner + place, 0)
        greet(g * inner + place, 1)

    waits = 2 * inner - 1 + 2 * (outer - 1 - group)
    if not last:

        @pl.when(here > 0)
        def _():
            greet(here - 1, core)

        waits = waits + jnp.where(here < count - 1, 1, 0)
    pl.semaphore_wait(barrier, waits)

    others(lambda i, c: inside(i, c).start())
    if not last:

        @pl.when(here < count - 1)
        def _():
            neighbour().start()

        @pl.when(here == 0)
        def _():
            mix_in[...] = jnp.zeros_like(mix_in)

    held[place, core] = d_ref[...]

    def arrive_inside(i, c):
        copy(
            d_ref, held.at[i, c], send_a.at[i, c], recv_a.at[i, c], start + i, c
        ).wait_recv()

    others(arrive_inside)
    total = jnp.zeros(d_ref.shape, F32)
    for i in range(inner):
        total = total + held[i, core].astype(F32)
    mine[...] = total.astype(BF16)

    @pl.loop(group + 1, outer)
    def _(g):
        onward(g, 0).start()
        onward(g, 1).start()

    def partial(c):
        def add(i, acc):
            return acc + held[i, c].astype(F32)

        return lax.fori_loop(0, place, add, jnp.zeros(d_ref.shape, F32))

    before = [partial(core), partial(1 - core)]

    @pl.loop(0, group)
    def _(g):
        for c in range(2):
            copy(
                mine,
                totals.at[g, c],
                send_b.at[g, c],
                recv_b.at[g, c],
                g * inner + place,
                c,
            ).wait_recv()

    def gather(c, acc):
        return lax.fori_loop(0, group, lambda g, a: a + totals[g, c].astype(F32), acc)

    before = [gather(core, before[0]), gather(1 - core, before[1])]
    own = held[place, core].astype(F32)
    other = held[place, 1 - core].astype(F32)
    sums = [before[0] + own, before[1] + other]
    noise = [noise_ref[0], noise_ref[1]]
    half = d_ref.shape[1]
    scale = 1.0 / (2 * d_ref.shape[0] * half)

    def mean_square(values):
        total = sum(v * v for v in values)
        total = jnp.sum(jnp.sum(total, axis=1, keepdims=True), axis=0, keepdims=True)
        return total * scale

    mix = mix_ref[0:1, 0:1]
    if last:
        old = [sums_in[0], sums_in[1]]
        state = [n + (1.0 + mix) * o for n, o in zip(noise, old)]
        picard = [n + s for n, s in zip(noise, sums)]
        second = mean_square([g - s for g, s in zip(picard, state)])
        res_ref[...] = jnp.concatenate([res_in[0:1, 0:1], second], axis=1)
        mix = mix_ref[1:2, 0:1]
        new = [g + mix * (s - o) for g, s, o in zip(picard, sums, old)]
        first = core == 0
        low, high = jnp.where(first, new[0], new[1]), jnp.where(first, new[1], new[0])
        blocks = [v[:, i : i + LANES] for v in (low, high) for i in range(0, half, LANES)]
        state_ref[...] = jnp.concatenate(blocks, axis=0).T
    else:
        sums_out[0] = sums[0]
        sums_out[1] = sums[1]
        res_ref[...] = jnp.broadcast_to(mean_square(sums), res_ref.shape)

        @pl.when(here > 0)
        def _():
            copy(mix_ref, mix_in, send_m.at[0], recv_m.at[0], here - 1, core).wait_recv()

        mix = 1.0 + mix_in[0:1, 0:1]
        x_ref[:, :half] = noise[0] + mix * before[0]
        x_ref[:, half:] = noise[1] + mix * before[1]

        @pl.when(here < count - 1)
        def _():
            neighbour().wait_send()

    others(lambda i, c: inside(i, c).wait_send())

    @pl.loop(group + 1, outer)
    def _(g):
        onward(g, 0).wait_send()
        onward(g, 1).wait_send()


def run_attention(x, patch, tables, mods, q_w, kv_w, out_w, rows_own):
    width = q_w.shape[0]
    seq = x.shape[1]
    tile = 256
    flops = 2 * seq * width * 2 * width + 4 * rows_own * width * width + 16 * rows_own * seq * width
    return pl.pallas_call(
        functools.partial(attention_kernel, tile),
        out_shape=jax.ShapeDtypeStruct((rows_own, width), F32),
        in_specs=[VM] * 7 + [ANY] * 3,
        out_specs=VM,
        scratch_shapes=[
            pltpu.VMEM((seq, width), BF16),
            pltpu.VMEM((seq, 2 * width), BF16),
            pltpu.VMEM((rows_own, width), BF16),
            pltpu.VMEM((rows_own, width), BF16),
            pltpu.VMEM((seq, 4 * HEAD_DIM), BF16),
            pltpu.VMEM(q_w.shape, BF16),
            pltpu.VMEM(kv_w.shape, BF16),
            pltpu.VMEM(out_w.shape, BF16),
            pltpu.SemaphoreType.DMA((3,)),
        ],
        compiler_params=pltpu.CompilerParams(vmem_limit_bytes=LIMIT),
        cost_estimate=pl.CostEstimate(
            flops=flops, bytes_accessed=8_000_000, transcendentals=rows_own * seq * width // 64
        ),
        name="attention",
    )(x, patch, *tables, mods, q_w, kv_w, out_w)


def run_mlp(coefs, x_own, h, mods, final_t, up_a, up_b, down_a, down_b):
    rows_own, width = h.shape
    units = up_a.shape[1]
    return pl.pallas_call(
        functools.partial(mlp_kernel, 256, 512),
        out_shape=jax.ShapeDtypeStruct((final_t.shape[0], rows_own), BF16),
        in_specs=[VM] * 5 + [ANY] * 4,
        out_specs=VM,
        scratch_shapes=[
            pltpu.VMEM((rows_own, width), BF16),
            pltpu.VMEM((rows_own, width), F32),
            pltpu.VMEM((2, width, units), BF16),
            pltpu.VMEM((2, units, width), BF16),
            pltpu.SemaphoreType.DMA((4,)),
        ],
        compiler_params=pltpu.CompilerParams(vmem_limit_bytes=LIMIT),
        cost_estimate=pl.CostEstimate(
            flops=8 * rows_own * width * units, bytes_accessed=12_000_000, transcendentals=0
        ),
        name="feed_forward",
    )(coefs, x_own, h, mods, final_t, up_a, up_b, down_a, down_b)


def run_prefix(count, drift, noise, mix, *carried):
    part = drift.shape
    inner = 1
    while inner * inner < count:
        inner *= 2
    last = bool(carried)
    both = jax.ShapeDtypeStruct((2,) + part, F32)
    flat = jax.ShapeDtypeStruct((part[0], 2 * part[1]), F32)
    square = jax.ShapeDtypeStruct((2 * part[0] * part[1] // LANES, LANES), F32)
    ends = jax.ShapeDtypeStruct((1, 2), F32)
    small = jax.ShapeDtypeStruct((8, 128), F32)
    return pl.pallas_call(
        functools.partial(prefix_kernel, count, inner, last),
        out_shape=(square, ends) if last else (both, flat, small),
        in_specs=[VM] * (5 if last else 3),
        out_specs=(VM,) * (2 if last else 3),
        scratch_shapes=[
            pltpu.VMEM((inner, 2) + part, BF16),
            pltpu.VMEM((count // inner, 2) + part, BF16),
            pltpu.VMEM(part, BF16),
            pltpu.VMEM((8, 128), F32),
            pltpu.SemaphoreType.DMA((inner, 2)),
            pltpu.SemaphoreType.DMA((inner, 2)),
            pltpu.SemaphoreType.DMA((count // inner, 2)),
            pltpu.SemaphoreType.DMA((count // inner, 2)),
            pltpu.SemaphoreType.DMA((1,)),
            pltpu.SemaphoreType.DMA((1,)),
        ],
        compiler_params=pltpu.CompilerParams(
            collective_id=1 if last else 0, has_side_effects=True
        ),
        name="prefix_last" if last else "prefix",
    )(drift, noise, mix, *carried)


def run_setup(patch, times, label, noise, mixing, table, time_in, time_out, ada, final_ada):
    seq = noise.size // patch
    width = time_out.shape[0]
    small = jax.ShapeDtypeStruct((8, 128), F32)
    return pl.pallas_call(
        setup_kernel,
        out_shape=(
            jax.ShapeDtypeStruct((8, width), F32),
            small,
            small,
            jax.ShapeDtypeStruct((2, patch, seq // 2), F32),
            jax.ShapeDtypeStruct((patch, seq), F32),
        ),
        in_specs=[SM, SM, VM, SM] + [ANY] * 5,
        out_specs=(VM,) * 5,
        scratch_shapes=[
            pltpu.VMEM((8, width), BF16),
            pltpu.VMEM(time_in.shape, BF16),
            pltpu.VMEM(time_out.shape, BF16),
            pltpu.VMEM(ada.shape, BF16),
            pltpu.VMEM(final_ada.shape, BF16),
            pltpu.SemaphoreType.DMA((11,)),
        ],
        compiler_params=pltpu.CompilerParams(vmem_limit_bytes=LIMIT),
        cost_estimate=pl.CostEstimate(flops=0, bytes_accessed=12_000_000, transcendentals=0),
        name="setup",
    )(times, label, noise, mixing, table, time_in, time_out, ada, final_ada)


def per_device(
    noise_start,
    timesteps,
    class_labels,
    mixing,
    class_table,
    time_in,
    time_out,
    ada_weight,
    final_ada,
    patch_weight,
    q_weight,
    kv_weight,
    out_weight,
    up_weight,
    down_weight,
    final_weight,
):
    count = lax.axis_size("tm")
    patch, width = patch_weight.shape
    seq = noise_start.shape[1] // patch
    rows_own = seq // 2
    swap = [(0, 1), (1, 0)]
    up_other = lax.ppermute(up_weight, "tensor", swap)
    down_other = lax.ppermute(down_weight, "tensor", swap)

    mods, coefs, mix, noise, x = run_setup(
        patch,
        timesteps,
        class_labels,
        noise_start.reshape(noise_start.size // LANES, LANES),
        mixing.T,
        class_table,
        time_in,
        time_out,
        ada_weight,
        final_ada,
    )

    half_width = width // 2
    rates = np.exp(-math.log(10000.0) * np.arange(half_width) / half_width)[None]
    spans = LANES // patch
    far = spans * np.arange(seq // spans)[:, None] * rates
    near = np.arange(spans)[:, None] * rates
    tables = [
        jnp.asarray(t.astype(np.float32))
        for t in (np.sin(far), np.cos(far), np.sin(near), np.cos(near))
    ]
    final_t = final_weight.T

    def drift_of(x):
        h = run_attention(
            x, patch_weight, tables, mods, q_weight, kv_weight, out_weight, rows_own
        )
        return run_mlp(coefs, x, h, mods, final_t, up_weight, up_other, down_weight, down_other)

    sums, x, first = run_prefix(count, drift_of(x), noise, mix)
    state, residuals = run_prefix(count, drift_of(x), noise, mix, sums, first)
    return (state.reshape((1,) + noise_start.shape), residuals.T)


def solution(mesh):
    in_specs = (
        P(),
        P(),
        P("tm", None),
        P(None, "tm"),
        P(),
        P(),
        P(),
        P(),
        P(),
        P(),
        P(),
        P(),
        P(),
        P(None, "tensor"),
        P("tensor", None),
        P(),
    )
    out_specs = (P("tm", None, None), P(None, "tm"))
    return jax.shard_map(
        per_device, mesh=mesh, in_specs=in_specs, out_specs=out_specs, check_vma=False
    )
```

```python
import functools
import math

import jax
import jax.numpy as jnp
from jax import lax
from jax.experimental import pallas as pl
from jax.experimental.pallas import tpu as pltpu
from jax.sharding import PartitionSpec as P
import numpy as np

HEAD_DIM = 64
ITERS = 2
LANES = 128
norm_eps = 1e-06
plan_steps = 1000
MESH = pl.DeviceIdType.MESH
F32 = jnp.float32
BF16 = jnp.bfloat16
ANY = pl.BlockSpec(memory_space=pl.ANY)
VM = pl.BlockSpec(memory_space=pltpu.VMEM)
SM = pl.BlockSpec(memory_space=pltpu.SMEM)
LIMIT = 62 * 1024 * 1024


def normed(values):
    center = values - jnp.mean(values, axis=-1, keepdims=True)
    spread = jnp.mean(center * center, axis=-1, keepdims=True)
    return center * lax.rsqrt(spread + norm_eps)


def attention_kernel(
    tile,
    x_ref,
    patch_ref,
    far_sin,
    far_cos,
    near_sin,
    near_cos,
    mod_ref,
    q_hbm,
    kv_hbm,
    out_hbm,
    h_ref,
    in_s,
    kv_s,
    q_s,
    att_s,
    value_s,
    q_w,
    kv_w,
    out_w,
    sems,
):
    rows_own, width = h_ref.shape
    seq = x_ref.shape[1]
    copies = [
        pltpu.make_async_copy(src, dst, sems.at[i])
        for i, (src, dst) in enumerate(((kv_hbm, kv_w), (q_hbm, q_w), (out_hbm, out_w)))
    ]
    for copy in copies:
        copy.start()
    shift, scale, gate = mod_ref[0:1, :], 1.0 + mod_ref[1:2, :], mod_ref[2:3, :]
    lines = far_sin.shape[0]
    spans = seq // lines
    member = lax.axis_index("tensor")
    fs, fc = far_sin[...], far_cos[...]

    def embed(t):
        rows = slice(t * tile, (t + 1) * tile)
        hidden = lax.dot_general(
            x_ref[:, rows].astype(BF16),
            patch_ref[...],
            (((0,), (0,)), ((), ())),
            preferred_element_type=F32,
        )
        blocks = []
        for i in range(tile // lines):
            turn = lax.rem(t * (tile // lines) + i + member * (spans // 2), spans)
            ns, nc = near_sin[pl.ds(turn, 1), :], near_cos[pl.ds(turn, 1), :]
            blocks.append(jnp.concatenate([fs * nc + fc * ns, fc * nc - fs * ns], axis=1))
        hidden = hidden + jnp.concatenate(blocks, axis=0)
        if t * tile < rows_own:
            h_ref[rows, :] = hidden
        in_s[rows, :] = (normed(hidden) * scale + shift).astype(BF16)

    def project(t):
        rows = slice(t * tile, (t + 1) * tile)
        attn_in = in_s[rows, :]
        kv_s[rows, :] = jnp.dot(attn_in, kv_w[...], preferred_element_type=F32).astype(BF16)
        if t * tile < rows_own:
            q = jnp.dot(attn_in, q_w[...], preferred_element_type=F32).astype(BF16)
            q_s[rows, :] = q * BF16(1.0 / math.sqrt(HEAD_DIM))

    pair = 2 * HEAD_DIM
    value_s[:, pair:] = jnp.ones((seq, pair), BF16)
    embed(0)
    copies[0].wait()
    copies[1].wait()
    for t in range(seq // tile):
        if (t + 1) * tile < seq:
            embed(t + 1)
        project(t)

    first = lax.broadcasted_iota(jnp.int32, (tile, pair), 1) < HEAD_DIM

    @pl.loop(0, width // pair)
    def _(hp):
        cols = pl.ds(pl.multiple_of(hp * pair, pair), pair)
        keys = kv_s[:, cols]
        value_s[:, :pair] = kv_s[:, pl.ds(pl.multiple_of(width + hp * pair, pair), pair)]
        values = value_s[...]
        for t in range(rows_own // tile):
            rows = slice(t * tile, (t + 1) * tile)
            q2 = q_s[rows, cols]
            outs = []
            for mask in (first, jnp.logical_not(first)):
                s = lax.dot_general(
                    jnp.where(mask, q2, BF16(0)),
                    keys,
                    (((1,), (1,)), ((), ())),
                    preferred_element_type=F32,
                )
                p = jnp.exp(s - jnp.max(s, axis=-1, keepdims=True)).astype(BF16)
                o = jnp.dot(p, values, preferred_element_type=F32)
                outs.append(o[:, :pair] / o[:, pair:])
            att_s[rows, cols] = jnp.where(first, outs[0], outs[1]).astype(BF16)

    copies[2].wait()

    @pl.loop(0, rows_own // tile)
    def _(t):
        rows = pl.ds(pl.multiple_of(t * tile, tile), tile)
        h_ref[rows, :] += gate * jnp.dot(att_s[rows, :], out_w[...], preferred_element_type=F32)


def mlp_kernel(
    tile,
    block,
    coef_ref,
    x_ref,
    h_ref,
    mod_ref,
    final_ref,
    up_a,
    up_b,
    down_a,
    down_b,
    d_ref,
    in_s,
    sum_s,
    up_w,
    down_w,
    sems,
):
    rows_own, width = h_ref.shape
    hidden_units = up_w.shape[2]
    copies = []
    for i, (src, dst) in enumerate(
        ((up_a, up_w.at[0]), (down_a, down_w.at[0]), (up_b, up_w.at[1]), (down_b, down_w.at[1]))
    ):
        copy = pltpu.make_async_copy(src, dst, sems.at[i])
        copy.start()
        copies.append(copy)
    shift, scale, gate = mod_ref[3:4, :], 1.0 + mod_ref[4:5, :], mod_ref[5:6, :]
    shift_o, scale_o = mod_ref[6:7, :], 1.0 + mod_ref[7:8, :]
    keep, noise = coef_ref[0:1, 0:1], coef_ref[1:2, 0:1]
    tiles = rows_own // tile

    def rows_of(t):
        return pl.ds(pl.multiple_of(t * tile, tile), tile)

    @pl.loop(0, tiles)
    def _(t):
        in_s[rows_of(t), :] = (normed(h_ref[rows_of(t), :]) * scale + shift).astype(BF16)

    for half in range(2):
        copies[2 * half].wait()
        copies[2 * half + 1].wait()

        @pl.loop(0, tiles)
        def _(t):
            rows = rows_of(t)
            x = in_s[rows, :]
            acc = jnp.zeros((tile, width), F32)
            for j in range(hidden_units // block):
                part = slice(j * block, (j + 1) * block)
                lifted = jnp.dot(x, up_w[half, :, part], preferred_element_type=F32)
                lifted = jax.nn.gelu(lifted, approximate=True).astype(BF16)
                acc = acc + jnp.dot(lifted, down_w[half, part, :], preferred_element_type=F32)
            acc = acc.astype(BF16).astype(F32)
            if half == 0:
                sum_s[rows, :] = acc
            else:
                h2 = h_ref[rows, :] + gate * (sum_s[rows, :] + acc)
                final_in = (normed(h2) * scale_o + shift_o).astype(BF16)
                eps = lax.dot_general(
                    final_ref[...], final_in, (((1,), (1,)), ((), ())), preferred_element_type=F32
                )
                d_ref[:, rows] = (keep * x_ref[:, rows] + noise * eps).astype(BF16)


def setup_kernel(
    times_ref,
    label_ref,
    noise_ref,
    mixing_ref,
    table_hbm,
    in_hbm,
    out_hbm,
    ada_hbm,
    final_hbm,
    mod_ref,
    coef_ref,
    mix_ref,
    halves_ref,
    x_ref,
    rows_v,
    in_v,
    out_v,
    ada_v,
    final_v,
    sems,
):
    here = lax.axis_index("tm")
    member = lax.axis_index("tensor")
    label = label_ref[0, 0]
    width = mod_ref.shape[1]
    base = pl.multiple_of(label // 8 * 8, 8)
    copies = []

    def begin(src, dst):
        copy = pltpu.make_async_copy(src, dst, sems.at[len(copies)])
        copy.start()
        copies.append(copy)

    begin(in_hbm, in_v)
    begin(out_hbm, out_v)
    begin(table_hbm.at[pl.ds(base, 8), :], rows_v)
    parts = []
    for src, dst in ((ada_hbm, ada_v), (final_hbm, final_v)):
        for j in range(src.shape[1] // width):
            cols = slice(j * width, (j + 1) * width)
            begin(src.at[:, cols], dst.at[:, cols])
            parts.append(dst.at[:, cols])

    level = lax.broadcasted_iota(jnp.int32, (8, 128), 0) * 128
    level = level + lax.broadcasted_iota(jnp.int32, (8, 128), 1)
    beta = 0.0001 + (0.02 - 0.0001) * level.astype(F32) / (plan_steps - 1)
    logs = jnp.log(1.0 - beta)
    now = times_ref[here]

    def alpha(moment):
        kept = jnp.where(level <= moment, logs, 0.0)
        total = jnp.sum(jnp.sum(kept, axis=1, keepdims=True), axis=0, keepdims=True)
        return jnp.exp(total)

    before, after = alpha(now), alpha(times_ref[here + 1])
    keep = jnp.sqrt(after / before) - 1.0
    noise = jnp.sqrt(1.0 - after) - jnp.sqrt(after * (1.0 - before) / before)
    coef_ref[0:1, :] = jnp.broadcast_to(keep, (1, 128))
    coef_ref[1:2, :] = jnp.broadcast_to(noise, (1, 128))
    coef_ref[2:8, :] = jnp.zeros((6, 128), F32)
    mix_ref[0:1, :] = jnp.full((1, 128), mixing_ref[0, 0], F32)
    mix_ref[1:2, :] = jnp.full((1, 128), mixing_ref[0, 1], F32)
    mix_ref[2:8, :] = jnp.zeros((6, 128), F32)

    turned = noise_ref[...].T
    patch = x_ref.shape[0]
    blocks = turned.shape[0] // patch // 2
    low = [turned[i * patch : (i + 1) * patch] for i in range(blocks)]
    high = [turned[(blocks + i) * patch : (blocks + i + 1) * patch] for i in range(blocks)]
    left, right = jnp.concatenate(low, axis=1), jnp.concatenate(high, axis=1)
    half = left.shape[1]
    first = member == 0
    own, other = jnp.where(first, left, right), jnp.where(first, right, left)
    halves_ref[0] = own
    halves_ref[1] = other
    x_ref[:, :half] = own
    x_ref[:, half:] = other

    count = in_v.shape[0] // 2
    lane = lax.broadcasted_iota(jnp.int32, (8, count), 1).astype(F32)
    angle = now.astype(F32) * jnp.exp(-math.log(10000.0) * lane / count)
    features = jnp.concatenate([jnp.cos(angle), jnp.sin(angle)], axis=1).astype(BF16)
    copies[0].wait()
    hidden = jax.nn.silu(jnp.dot(features, in_v[...], preferred_element_type=F32)).astype(BF16)
    copies[1].wait()
    embed = jnp.dot(hidden, out_v[...], preferred_element_type=F32)
    copies[2].wait()
    picked = lax.broadcasted_iota(jnp.int32, (8, width), 0) == label - base
    entry = jnp.sum(jnp.where(picked, rows_v[...].astype(F32), 0.0), axis=0, keepdims=True)
    cond = jax.nn.silu(embed + entry).astype(BF16)
    for j, part in enumerate(parts):
        copies[3 + j].wait()
        mod_ref[j : j + 1, :] = jnp.dot(cond, part[...], preferred_element_type=F32)[0:1, :]


def prefix_kernel(
    count,
    inner,
    last,
    d_ref,
    noise_ref,
    mix_ref,
    *rest,
):
    if last:
        sums_in, res_in, state_ref, res_ref, *rest = rest
    else:
        sums_out, x_ref, res_ref, *rest = rest
    held, totals, mine, mix_in, send_a, recv_a, send_b, recv_b, send_m, recv_m = rest
    here = lax.axis_index("tm")
    core = lax.axis_index("tensor")
    outer = count // inner
    group, place = here // inner, here % inner
    start = group * inner

    def copy(src, dst, send, recv, target, target_core):
        return pltpu.make_async_remote_copy(
            src_ref=src,
            dst_ref=dst,
            send_sem=send,
            recv_sem=recv,
            device_id=(target, target_core),
            device_id_type=MESH,
        )

    def inside(i, c):
        return copy(
            d_ref, held.at[place, core], send_a.at[i, c], recv_a.at[place, core], start + i, c
        )

    def onward(g, c):
        return copy(
            mine,
            totals.at[group, core],
            send_b.at[g, c],
            recv_b.at[group, core],
            g * inner + place,
            c,
        )

    def neighbour():
        return copy(mix_ref, mix_in, send_m.at[0], recv_m.at[0], here + 1, core)

    barrier = pltpu.get_barrier_semaphore()

    def greet(target, c):
        pl.semaphore_signal(barrier, inc=1, device_id=(target, c), device_id_type=MESH)

    def others(act):
        act(place, 1 - core)

        @pl.loop(1, inner)
        def _(step):
            i = lax.rem(place + step, inner)
            act(i, 0)
            act(i, 1)

    others(lambda i, c: greet(start + i, c))

    @pl.loop(0, group)
    def _(g):
        greet(g * inner + place, 0)
        greet(g * inner + place, 1)

    waits = 2 * inner - 1 + 2 * (outer - 1 - group)
    if not last:

        @pl.when(here > 0)
        def _():
            greet(here - 1, core)

        waits = waits + jnp.where(here < count - 1, 1, 0)
    pl.semaphore_wait(barrier, waits)

    others(lambda i, c: inside(i, c).start())
    if not last:

        @pl.when(here < count - 1)
        def _():
            neighbour().start()

        @pl.when(here == 0)
        def _():
            mix_in[...] = jnp.zeros_like(mix_in)

    held[place, core] = d_ref[...]

    def arrive_inside(i, c):
        copy(
            d_ref, held.at[i, c], send_a.at[i, c], recv_a.at[i, c], start + i, c
        ).wait_recv()

    others(arrive_inside)
    total = jnp.zeros(d_ref.shape, F32)
    for i in range(inner):
        total = total + held[i, core].astype(F32)
    mine[...] = total.astype(BF16)

    @pl.loop(group + 1, outer)
    def _(g):
        onward(g, 0).start()
        onward(g, 1).start()

    def partial(c):
        def add(i, acc):
            return acc + held[i, c].astype(F32)

        return lax.fori_loop(0, place, add, jnp.zeros(d_ref.shape, F32))

    before = [partial(core), partial(1 - core)]

    @pl.loop(0, group)
    def _(g):
        for c in range(2):
            copy(
                mine,
                totals.at[g, c],
                send_b.at[g, c],
                recv_b.at[g, c],
                g * inner + place,
                c,
            ).wait_recv()

    def gather(c, acc):
        return lax.fori_loop(0, group, lambda g, a: a + totals[g, c].astype(F32), acc)

    before = [gather(core, before[0]), gather(1 - core, before[1])]
    own = held[place, core].astype(F32)
    other = held[place, 1 - core].astype(F32)
    sums = [before[0] + own, before[1] + other]
    noise = [noise_ref[0], noise_ref[1]]
    half = d_ref.shape[1]
    scale = 1.0 / (2 * d_ref.shape[0] * half)

    def mean_square(values):
        total = sum(v * v for v in values)
        total = jnp.sum(jnp.sum(total, axis=1, keepdims=True), axis=0, keepdims=True)
        return total * scale

    mix = mix_ref[0:1, 0:1]
    if last:
        old = [sums_in[0], sums_in[1]]
        state = [n + (1.0 + mix) * o for n, o in zip(noise, old)]
        picard = [n + s for n, s in zip(noise, sums)]
        second = mean_square([g - s for g, s in zip(picard, state)])
        res_ref[...] = jnp.concatenate([res_in[0:1, 0:1], second], axis=1)
        mix = mix_ref[1:2, 0:1]
        new = [g + mix * (s - o) for g, s, o in zip(picard, sums, old)]
        first = core == 0
        low, high = jnp.where(first, new[0], new[1]), jnp.where(first, new[1], new[0])
        blocks = [v[:, i : i + LANES] for v in (low, high) for i in range(0, half, LANES)]
        state_ref[...] = jnp.concatenate(blocks, axis=0).T
    else:
        sums_out[0] = sums[0]
        sums_out[1] = sums[1]
        res_ref[...] = jnp.broadcast_to(mean_square(sums), res_ref.shape)

        @pl.when(here > 0)
        def _():
            copy(mix_ref, mix_in, send_m.at[0], recv_m.at[0], here - 1, core).wait_recv()

        mix = 1.0 + mix_in[0:1, 0:1]
        x_ref[:, :half] = noise[0] + mix * before[0]
        x_ref[:, half:] = noise[1] + mix * before[1]

        @pl.when(here < count - 1)
        def _():
            neighbour().wait_send()

    others(lambda i, c: inside(i, c).wait_send())

    @pl.loop(group + 1, outer)
    def _(g):
        onward(g, 0).wait_send()
        onward(g, 1).wait_send()


def run_attention(x, patch, tables, mods, q_w, kv_w, out_w, rows_own):
    width = q_w.shape[0]
    seq = x.shape[1]
    tile = 256
    flops = 2 * seq * width * 2 * width + 4 * rows_own * width * width + 16 * rows_own * seq * width
    return pl.pallas_call(
        functools.partial(attention_kernel, tile),
        out_shape=jax.ShapeDtypeStruct((rows_own, width), F32),
        in_specs=[VM] * 7 + [ANY] * 3,
        out_specs=VM,
        scratch_shapes=[
            pltpu.VMEM((seq, width), BF16),
            pltpu.VMEM((seq, 2 * width), BF16),
            pltpu.VMEM((rows_own, width), BF16),
            pltpu.VMEM((rows_own, width), BF16),
            pltpu.VMEM((seq, 4 * HEAD_DIM), BF16),
            pltpu.VMEM(q_w.shape, BF16),
            pltpu.VMEM(kv_w.shape, BF16),
            pltpu.VMEM(out_w.shape, BF16),
            pltpu.SemaphoreType.DMA((3,)),
        ],
        compiler_params=pltpu.CompilerParams(vmem_limit_bytes=LIMIT),
        cost_estimate=pl.CostEstimate(
            flops=flops, bytes_accessed=8_000_000, transcendentals=rows_own * seq * width // 64
        ),
        name="attention",
    )(x, patch, *tables, mods, q_w, kv_w, out_w)


def run_mlp(coefs, x_own, h, mods, final_t, up_a, up_b, down_a, down_b):
    rows_own, width = h.shape
    units = up_a.shape[1]
    return pl.pallas_call(
        functools.partial(mlp_kernel, 512, 512),
        out_shape=jax.ShapeDtypeStruct((final_t.shape[0], rows_own), BF16),
        in_specs=[VM] * 5 + [ANY] * 4,
        out_specs=VM,
        scratch_shapes=[
            pltpu.VMEM((rows_own, width), BF16),
            pltpu.VMEM((rows_own, width), F32),
            pltpu.VMEM((2, width, units), BF16),
            pltpu.VMEM((2, units, width), BF16),
            pltpu.SemaphoreType.DMA((4,)),
        ],
        compiler_params=pltpu.CompilerParams(vmem_limit_bytes=LIMIT),
        cost_estimate=pl.CostEstimate(
            flops=8 * rows_own * width * units, bytes_accessed=12_000_000, transcendentals=0
        ),
        name="feed_forward",
    )(coefs, x_own, h, mods, final_t, up_a, up_b, down_a, down_b)


def run_prefix(count, drift, noise, mix, *carried):
    part = drift.shape
    inner = 1
    while inner * inner < count:
        inner *= 2
    last = bool(carried)
    both = jax.ShapeDtypeStruct((2,) + part, F32)
    flat = jax.ShapeDtypeStruct((part[0], 2 * part[1]), F32)
    square = jax.ShapeDtypeStruct((2 * part[0] * part[1] // LANES, LANES), F32)
    ends = jax.ShapeDtypeStruct((1, 2), F32)
    small = jax.ShapeDtypeStruct((8, 128), F32)
    return pl.pallas_call(
        functools.partial(prefix_kernel, count, inner, last),
        out_shape=(square, ends) if last else (both, flat, small),
        in_specs=[VM] * (5 if last else 3),
        out_specs=(VM,) * (2 if last else 3),
        scratch_shapes=[
            pltpu.VMEM((inner, 2) + part, BF16),
            pltpu.VMEM((count // inner, 2) + part, BF16),
            pltpu.VMEM(part, BF16),
            pltpu.VMEM((8, 128), F32),
            pltpu.SemaphoreType.DMA((inner, 2)),
            pltpu.SemaphoreType.DMA((inner, 2)),
            pltpu.SemaphoreType.DMA((count // inner, 2)),
            pltpu.SemaphoreType.DMA((count // inner, 2)),
            pltpu.SemaphoreType.DMA((1,)),
            pltpu.SemaphoreType.DMA((1,)),
        ],
        compiler_params=pltpu.CompilerParams(
            collective_id=1 if last else 0, has_side_effects=True
        ),
        name="prefix_last" if last else "prefix",
    )(drift, noise, mix, *carried)


def run_setup(patch, times, label, noise, mixing, table, time_in, time_out, ada, final_ada):
    seq = noise.size // patch
    width = time_out.shape[0]
    small = jax.ShapeDtypeStruct((8, 128), F32)
    return pl.pallas_call(
        setup_kernel,
        out_shape=(
            jax.ShapeDtypeStruct((8, width), F32),
            small,
            small,
            jax.ShapeDtypeStruct((2, patch, seq // 2), F32),
            jax.ShapeDtypeStruct((patch, seq), F32),
        ),
        in_specs=[SM, SM, VM, SM] + [ANY] * 5,
        out_specs=(VM,) * 5,
        scratch_shapes=[
            pltpu.VMEM((8, width), BF16),
            pltpu.VMEM(time_in.shape, BF16),
            pltpu.VMEM(time_out.shape, BF16),
            pltpu.VMEM(ada.shape, BF16),
            pltpu.VMEM(final_ada.shape, BF16),
            pltpu.SemaphoreType.DMA((11,)),
        ],
        compiler_params=pltpu.CompilerParams(vmem_limit_bytes=LIMIT),
        cost_estimate=pl.CostEstimate(flops=0, bytes_accessed=12_000_000, transcendentals=0),
        name="setup",
    )(times, label, noise, mixing, table, time_in, time_out, ada, final_ada)


def per_device(
    noise_start,
    timesteps,
    class_labels,
    mixing,
    class_table,
    time_in,
    time_out,
    ada_weight,
    final_ada,
    patch_weight,
    q_weight,
    kv_weight,
    out_weight,
    up_weight,
    down_weight,
    final_weight,
):
    count = lax.axis_size("tm")
    patch, width = patch_weight.shape
    seq = noise_start.shape[1] // patch
    rows_own = seq // 2
    swap = [(0, 1), (1, 0)]
    up_other = lax.ppermute(up_weight, "tensor", swap)
    down_other = lax.ppermute(down_weight, "tensor", swap)

    mods, coefs, mix, noise, x = run_setup(
        patch,
        timesteps,
        class_labels,
        noise_start.reshape(noise_start.size // LANES, LANES),
        mixing.T,
        class_table,
        time_in,
        time_out,
        ada_weight,
        final_ada,
    )

    half_width = width // 2
    rates = np.exp(-math.log(10000.0) * np.arange(half_width) / half_width)[None]
    spans = LANES // patch
    far = spans * np.arange(seq // spans)[:, None] * rates
    near = np.arange(spans)[:, None] * rates
    tables = [
        jnp.asarray(t.astype(np.float32))
        for t in (np.sin(far), np.cos(far), np.sin(near), np.cos(near))
    ]
    final_t = final_weight.T

    def drift_of(x):
        h = run_attention(
            x, patch_weight, tables, mods, q_weight, kv_weight, out_weight, rows_own
        )
        return run_mlp(coefs, x, h, mods, final_t, up_weight, up_other, down_weight, down_other)

    sums, x, first = run_prefix(count, drift_of(x), noise, mix)
    state, residuals = run_prefix(count, drift_of(x), noise, mix, sums, first)
    return (state.reshape((1,) + noise_start.shape), residuals.T)


def solution(mesh):
    in_specs = (
        P(),
        P(),
        P("tm", None),
        P(None, "tm"),
        P(),
        P(),
        P(),
        P(),
        P(),
        P(),
        P(),
        P(),
        P(),
        P(None, "tensor"),
        P("tensor", None),
        P(),
    )
    out_specs = (P("tm", None, None), P(None, "tm"))
    return jax.shard_map(
        per_device, mesh=mesh, in_specs=in_specs, out_specs=out_specs, check_vma=False
    )
```
